32 devices in a mesh: dp: 8 (over y, x, core), tensor: 4 (over z).
Axes of the slice: x: 2, y: 2, z: 4, core: 2. Of those that a mesh axis runs over, the one named last changes fastest.
Arguments:
- block_input: bfloat16 [1536, 1536], P('dp'), may hold values from -6 to 6
- segments: int32 [1536], P('dp'), may hold values from 0 to 2, as said below
- positions: int32 [1536], P('dp'), may hold values from 0 to 191, as said below
- cotangent: bfloat16 [1536, 1536], P('dp'), may hold values from -6 to 6
- gain_attn: float32 [1536], replicated, may hold values from 0.1 to 1.9
- w_query: bfloat16 [1536, 1536], P(None, 'tensor'), may hold values from -0.15625 to 0.15625
- b_query: float32 [1536], P('tensor'), may hold values from -3 to 3
- w_key: bfloat16 [1536, 256], replicated, may hold values from -0.15625 to 0.15625
- b_key: float32 [256], replicated, may hold values from -3 to 3
- w_value: bfloat16 [1536, 256], replicated, may hold values from -0.15625 to 0.15625
- b_value: float32 [256], replicated, may hold values from -3 to 3
- w_out: bfloat16 [1536, 1536], P('tensor'), may hold values from -0.4375 to 0.4375
- gain_mlp: float32 [1536], replicated, may hold values from 0.1 to 1.9
- w_gate: bfloat16 [1536, 8960], P(None, 'tensor'), may hold values from -0.15625 to 0.15625
- w_up: bfloat16 [1536, 8960], P(None, 'tensor'), may hold values from -0.15625 to 0.15625
- w_down: bfloat16 [8960, 1536], P('tensor'), may hold values from -0.0625 to 0.0625
Outputs:
- output: float32 [1536, 1536], P('dp')
- d_input: float32 [1536, 1536], P('dp')
- grad_gain_attn: float32 [1536], replicated
- grad_w_query: float32 [1536, 1536], P('dp', 'tensor')
- grad_b_query: float32 [1536], replicated
- grad_w_key: float32 [1536, 256], P(('dp', 'tensor'))
- grad_b_key: float32 [256], replicated
- grad_w_value: float32 [1536, 256], P(('dp', 'tensor'))
- grad_b_value: float32 [256], replicated
- grad_w_out: float32 [1536, 1536], P('tensor', 'dp')
- grad_gain_mlp: float32 [1536], replicated
- grad_w_gate: float32 [1536, 8960], P('dp', 'tensor')
- grad_w_up: float32 [1536, 8960], P('dp', 'tensor')
- grad_w_down: float32 [8960, 1536], P('tensor', 'dp')
The draws below stay inside these ranges and needn't reach their ends.
Inputs may be any that keep to these rules, and one draw needn't show every extreme that they name: `segments`: within each packed sequence of 192 tokens the segment number starts at 0 and rises by one at each new document; each document holds 32 to 192 tokens. `positions`: each token's index within its document.
All inputs are finite; a program needn't handle non-finite values.
Results may differ from the reference program's by a relative error of at most 0.019.
The reference program's roundings to bfloat16 on the way count: a program that leaves them out, or rounds other values in their place, can miss the bound.
Values may be sent and summed in bfloat16 or wider, within the bound.
No kernel may reach another device: no remote copies, remote signals or barrier semaphores. Data moves between devices by JAX's collectives and lax.ppermute only.
A program may use at most 192 MiB of HBM per device.

```python
import math
import jax
import jax.numpy as jnp
from jax import lax

D = 1536
H = 12
KVH = 2
HD = 128
FF = 8960
SEQ = 192
TOKENS = 1536


def document_layout(key):
    base = jax.random.fold_in(key, 11)
    count_key, first_key, second_key = jax.random.split(base, 3)
    sequence_count = TOKENS // SEQ
    shortest = SEQ // 6
    document_count = jax.random.randint(count_key, (sequence_count,), 1, 4)
    document_count = document_count.at[0].set(3).at[1].set(1)
    first_high = jnp.where(document_count == 3, SEQ - 2 * shortest + 1, SEQ - shortest + 1)
    first_cut = jax.random.randint(first_key, (sequence_count,), shortest, first_high)
    second_low = jnp.minimum(first_cut + shortest, SEQ - shortest)
    second_cut = jax.random.randint(second_key, (sequence_count,), second_low, SEQ - shortest + 1)
    token_index = jnp.arange(SEQ)[None, :]
    in_second = (document_count[:, None] >= 2) & (token_index >= first_cut[:, None])
    in_third = (document_count[:, None] >= 3) & (token_index >= second_cut[:, None])
    segment_ids = in_second.astype(jnp.int32) + in_third.astype(jnp.int32)
    doc_start = jnp.where(in_third, second_cut[:, None], jnp.where(in_second, first_cut[:, None], 0))
    return (segment_ids.reshape(-1), (token_index - doc_start).reshape(-1).astype(jnp.int32))


def draw_segments(key, part):
    return document_layout(key)[0]


def draw_positions(key, part):
    return document_layout(key)[1]


def block_levels(own_key, shape, pieces, least, largest):
    level = 1.0
    for position, shards_of in pieces:
        draws = jax.random.uniform(jax.random.fold_in(jax.random.fold_in(own_key, 6), position), (shards_of,), jnp.float32, least / len(pieces), largest / len(pieces))
        level = level * jnp.repeat(jnp.exp(draws), shape[position] // shards_of).reshape((-1,) + (1,) * (len(shape) - 1 - position))
    return level


def normal_values(stream_key, dims, scale, most, pieces=(), kind=jnp.bfloat16):
    entries = jax.random.normal(stream_key, dims, jnp.float32) * scale
    if len(pieces) > 0:
        entries = block_levels(stream_key, dims, pieces, -0.22, 0.18) * entries
    return jnp.clip(entries, min=-most, max=most).astype(kind)


def setup_inputs(seed: int = 0) -> dict:
    key_of = jax.random.split(jax.random.key(seed), 17)
    return {
        "block_input": normal_values(key_of[0], (TOKENS, D), 1.0, 6.0, ((0, 8),)),
        "segments": draw_segments(jax.random.fold_in(key_of[16], 71), 0),
        "positions": draw_positions(jax.random.fold_in(key_of[16], 71), 0),
        "cotangent": normal_values(key_of[3], (TOKENS, D), 1.0, 6.0, ((0, 8),)),
        "gain_attn": jnp.clip(1.0 + 0.18 * jax.random.normal(key_of[4], (D,), jnp.float32), 0.1, 1.9),
        "w_query": normal_values(key_of[5], (D, H * HD), D ** -0.5, 0.15625, ((1, 4),)),
        "b_query": normal_values(key_of[6], (H * HD,), 0.5, 3.0, ((0, 4),), jnp.float32),
        "w_key": normal_values(key_of[7], (D, KVH * HD), D ** -0.5, 0.15625),
        "b_key": normal_values(key_of[8], (KVH * HD,), 0.5, 3.0, (), jnp.float32),
        "w_value": normal_values(key_of[9], (D, KVH * HD), D ** -0.5, 0.15625),
        "b_value": normal_values(key_of[10], (KVH * HD,), 0.5, 3.0, (), jnp.float32),
        "w_out": normal_values(key_of[11], (H * HD, D), (H * HD // 8) ** -0.5, 0.4375, ((0, 4),)),
        "gain_mlp": jnp.clip(1.0 + 0.18 * jax.random.normal(key_of[12], (D,), jnp.float32), 0.1, 1.9),
        "w_gate": normal_values(key_of[13], (D, FF), D ** -0.5, 0.15625, ((1, 4),)),
        "w_up": normal_values(key_of[14], (D, FF), D ** -0.5, 0.15625, ((1, 4),)),
        "w_down": normal_values(key_of[15], (FF, D), FF ** -0.5, 0.0625, ((0, 4),)),
    }


eps = 1e-06
theta = 1000000.0

def rope_tables(positions):
    exponent = jnp.arange(0, HD, 2).astype(jnp.float32) / HD
    frequency = jnp.power(jnp.float32(theta), -exponent)
    angles = positions.astype(jnp.float32)[:, None] * frequency[None, :]
    cosine = jnp.concatenate([jnp.cos(angles), jnp.cos(angles)], axis=1)
    sine_table = jnp.concatenate([jnp.sin(angles), jnp.sin(angles)], axis=1)
    return (cosine, sine_table)

def rotate(values):
    first_half = values[..., :HD // 2]
    second = values[..., HD // 2:]
    return jnp.concatenate([-second, first_half], axis=-1)

def rope_apply(values, cosine, sine_table):
    return values * cosine[:, None, :] + rotate(values) * sine_table[:, None, :]

def rope_back(gradient, cosine, sine_table):
    return gradient * cosine[:, None, :] - rotate(gradient * sine_table[:, None, :])

def norm_back(values, rscale, gain, upstream):
    scaled = gain * upstream
    return rscale * (scaled - values * rscale * rscale * lax.optimization_barrier(jnp.mean(scaled * values, axis=1, keepdims=True)))

def one_sequence(block_input, segments, positions, cotangent, weights):
    gain_attn, w_query, b_query, w_key, b_key, w_value, b_value, w_out, gain_mlp, w_gate, w_up, w_down = weights
    group = H // KVH
    score_scale = 1.0 / math.sqrt(HD)
    input_float = block_input.astype(jnp.float32)
    rscale_attn = lax.rsqrt(lax.optimization_barrier(jnp.mean(input_float * input_float, axis=1, keepdims=True)) + eps)
    normed_attn = (input_float * rscale_attn * gain_attn).astype(jnp.bfloat16)
    queries = jnp.dot(normed_attn, w_query, preferred_element_type=jnp.float32) + b_query
    keys_pre = jnp.dot(normed_attn, w_key, preferred_element_type=jnp.float32) + b_key
    values_pre = jnp.dot(normed_attn, w_value, preferred_element_type=jnp.float32) + b_value
    cosine, sine_table = rope_tables(positions)
    query_rot = rope_apply(queries.reshape(SEQ, H, HD), cosine, sine_table).astype(jnp.bfloat16)
    key_rot = rope_apply(keys_pre.reshape(SEQ, KVH, HD), cosine, sine_table).astype(jnp.bfloat16)
    value_heads = values_pre.reshape(SEQ, KVH, HD).astype(jnp.bfloat16)
    key_wide = jnp.repeat(key_rot, group, axis=1).astype(jnp.float32)
    value_wide = jnp.repeat(value_heads, group, axis=1).astype(jnp.float32)
    token_index = jnp.arange(SEQ)
    allowed = (segments[:, None] == segments[None, :]) & (token_index[None, :] <= token_index[:, None])
    scores = jnp.einsum('thd,uhd->htu', query_rot.astype(jnp.float32), key_wide) * score_scale
    masked = jnp.where(allowed[None], scores, -1e+30)
    row_top = lax.optimization_barrier(jnp.max(masked, axis=2, keepdims=True))
    log_total = row_top + jnp.log(lax.optimization_barrier(jnp.sum(jnp.exp(masked - row_top), axis=2, keepdims=True)))
    probabilities = jnp.exp(masked - log_total)
    rounded_probs = probabilities.astype(jnp.bfloat16)
    heads_out = jnp.einsum('htu,uhd->thd', rounded_probs.astype(jnp.float32), value_wide).astype(jnp.bfloat16)
    heads_flat = heads_out.reshape(SEQ, H * HD)
    hidden = input_float + jnp.dot(heads_flat, w_out, preferred_element_type=jnp.float32)
    rscale_mlp = lax.rsqrt(lax.optimization_barrier(jnp.mean(hidden * hidden, axis=1, keepdims=True)) + eps)
    normed_mlp = (hidden * rscale_mlp * gain_mlp).astype(jnp.bfloat16)
    gate_pre = jnp.dot(normed_mlp, w_gate, preferred_element_type=jnp.float32)
    up_pre = jnp.dot(normed_mlp, w_up, preferred_element_type=jnp.float32)
    sigmoid_gate = jax.nn.sigmoid(gate_pre)
    activated = (gate_pre * sigmoid_gate * up_pre).astype(jnp.bfloat16)
    output = hidden + jnp.dot(activated, w_down, preferred_element_type=jnp.float32)
    d_act = jnp.dot(cotangent, w_down.T, preferred_element_type=jnp.float32).astype(jnp.bfloat16)
    grad_down = jnp.dot(activated.T, cotangent, preferred_element_type=jnp.float32)
    act_float = d_act.astype(jnp.float32)
    d_gate = (act_float * up_pre * sigmoid_gate * (1.0 + gate_pre * (1.0 - sigmoid_gate))).astype(jnp.bfloat16)
    d_up = (act_float * gate_pre * sigmoid_gate).astype(jnp.bfloat16)
    grad_gate = jnp.dot(normed_mlp.T, d_gate, preferred_element_type=jnp.float32)
    grad_up = jnp.dot(normed_mlp.T, d_up, preferred_element_type=jnp.float32)
    d_normed_mlp = jnp.dot(d_gate, w_gate.T, preferred_element_type=jnp.float32) + jnp.dot(d_up, w_up.T, preferred_element_type=jnp.float32)
    grad_gain_mlp = lax.optimization_barrier(jnp.sum(d_normed_mlp * hidden * rscale_mlp, axis=0))
    d_hidden = cotangent.astype(jnp.float32) + norm_back(hidden, rscale_mlp, gain_mlp, d_normed_mlp)
    d_hidden_b = d_hidden.astype(jnp.bfloat16)
    grad_out = jnp.dot(heads_flat.T, d_hidden_b, preferred_element_type=jnp.float32)
    d_heads = jnp.dot(d_hidden_b, w_out.T, preferred_element_type=jnp.float32).astype(jnp.bfloat16).reshape(SEQ, H, HD)
    heads_float = d_heads.astype(jnp.float32)
    d_probs = jnp.einsum('thd,uhd->htu', heads_float, value_wide)
    delta = lax.optimization_barrier(jnp.sum(heads_float * heads_out.astype(jnp.float32), axis=2))
    d_scores = (probabilities * (d_probs - delta.T[:, :, None]) * score_scale).astype(jnp.bfloat16)
    scores_float = d_scores.astype(jnp.float32)
    d_qrot = jnp.einsum('htu,uhd->thd', scores_float, key_wide)
    d_krot = jnp.einsum('htu,thd->uhd', scores_float, query_rot.astype(jnp.float32))
    d_vhead = jnp.einsum('htu,thd->uhd', rounded_probs.astype(jnp.float32), heads_float)
    d_query = rope_back(d_qrot, cosine, sine_table)
    d_key = rope_back(d_krot, cosine, sine_table)
    grad_bq = lax.optimization_barrier(jnp.sum(d_query, axis=0)).reshape(H * HD)
    grad_bk = lax.optimization_barrier(jnp.sum(d_key.reshape(SEQ, KVH, group, HD), axis=(0, 2))).reshape(KVH * HD)
    grad_bv = lax.optimization_barrier(jnp.sum(d_vhead.reshape(SEQ, KVH, group, HD), axis=(0, 2))).reshape(KVH * HD)
    query_grad_b = d_query.astype(jnp.bfloat16).reshape(SEQ, H * HD)
    key_grad_b = d_key.astype(jnp.bfloat16).reshape(SEQ, KVH, group, HD).astype(jnp.float32)
    value_grad_b = d_vhead.astype(jnp.bfloat16).reshape(SEQ, KVH, group, HD).astype(jnp.float32)
    normed_float = normed_attn.astype(jnp.float32)
    grad_wq = jnp.dot(normed_attn.T, query_grad_b, preferred_element_type=jnp.float32)
    grad_wk = jnp.einsum('ud,ukge->dke', normed_float, key_grad_b).reshape(D, KVH * HD)
    grad_wv = jnp.einsum('ud,ukge->dke', normed_float, value_grad_b).reshape(D, KVH * HD)
    key_table = w_key.astype(jnp.float32).reshape(D, KVH, HD)
    value_table = w_value.astype(jnp.float32).reshape(D, KVH, HD)
    d_normed_attn = jnp.dot(query_grad_b, w_query.T, preferred_element_type=jnp.float32)
    d_normed_attn = d_normed_attn + jnp.einsum('ukge,dke->ud', key_grad_b, key_table)
    d_normed_attn = d_normed_attn + jnp.einsum('ukge,dke->ud', value_grad_b, value_table)
    grad_gain_attn = lax.optimization_barrier(jnp.sum(d_normed_attn * input_float * rscale_attn, axis=0))
    d_input = d_hidden + norm_back(input_float, rscale_attn, gain_attn, d_normed_attn)
    grads = (grad_gain_attn, grad_wq, grad_bq, grad_wk, grad_bk, grad_wv, grad_bv, grad_out, grad_gain_mlp, grad_gate, grad_up, grad_down)
    return (output, d_input, grads)

def reference(block_input, segments, positions, cotangent, gain_attn, w_query, b_query, w_key, b_key, w_value, b_value, w_out, gain_mlp, w_gate, w_up, w_down):
    weights = (gain_attn, w_query, b_query, w_key, b_key, w_value, b_value, w_out, gain_mlp, w_gate, w_up, w_down)
    sequence_count = TOKENS // SEQ
    inputs = (block_input.reshape(sequence_count, SEQ, D), segments.reshape(sequence_count, SEQ), positions.reshape(sequence_count, SEQ), cotangent.reshape(sequence_count, SEQ, D))
    initial = tuple((jnp.zeros(weight.shape, jnp.float32) for weight in weights))

    def advance(carry, item):
        output, d_input, grads = one_sequence(item[0], item[1], item[2], item[3], weights)
        return (tuple((running + extra for running, extra in zip(carry, grads))), (output, d_input))
    totals, (outputs, d_inputs) = lax.scan(advance, initial, inputs)
    return (outputs.reshape(TOKENS, D), d_inputs.reshape(TOKENS, D), totals[0], totals[1], totals[2], totals[3], totals[4], totals[5], totals[6], totals[7], totals[8], totals[9], totals[10], totals[11])
```

```python
import math

import jax
import jax.numpy as jnp
from jax import lax
from jax.sharding import PartitionSpec as P

D = 1536
H = 12
KVH = 2
HD = 128
SEQ = 192


eps = 1e-06
theta = 1000000.0


def rope_tables(positions):
    exponent = jnp.arange(0, HD, 2).astype(jnp.float32) / HD
    frequency = jnp.power(jnp.float32(theta), -exponent)
    angles = positions.astype(jnp.float32)[:, None] * frequency[None, :]
    cosine = jnp.concatenate([jnp.cos(angles), jnp.cos(angles)], axis=1)
    sine_table = jnp.concatenate([jnp.sin(angles), jnp.sin(angles)], axis=1)
    return (cosine, sine_table)


def rotate(values):
    first_half = values[..., : HD // 2]
    second = values[..., HD // 2 :]
    return jnp.concatenate([-second, first_half], axis=-1)


def rope_apply(values, cosine, sine_table):
    return values * cosine[:, None, :] + rotate(values) * sine_table[:, None, :]


def rope_back(gradient, cosine, sine_table):
    return gradient * cosine[:, None, :] - rotate(gradient * sine_table[:, None, :])


def norm_back(values, rscale, gain, upstream):
    scaled = gain * upstream
    return rscale * (
        scaled - values * rscale * rscale * jnp.mean(scaled * values, axis=1, keepdims=True)
    )


def swap(values, axis, step):
    size = lax.axis_size(axis)
    return lax.ppermute(values, axis, [(rank, rank ^ step) for rank in range(size)])


def token_order(values, rank, parts):
    size = values.shape[0] // parts
    return jnp.concatenate(
        [lax.dynamic_slice_in_dim(values, (rank ^ k) * size, size, 0) for k in range(parts)]
    )


def reduce_blocks(partial, axis):
    parts = lax.axis_size(axis)
    size = partial.shape[0] // parts
    sent = partial.astype(jnp.bfloat16)
    total = partial[:size]
    for k in range(1, parts):
        total = total + swap(sent[k * size : (k + 1) * size], axis, k).astype(jnp.float32)
    return total


def gather_blocks(own, axis):
    parts = lax.axis_size(axis)
    return [own] + [swap(own, axis, k) for k in range(1, parts)]


def gather_dp(own):
    parts = lax.axis_size("dp")
    blocks = {0: own}
    if parts == 8:
        half = own.shape[0] // 2
        blocks[2] = swap(own, "dp", 2)
        blocks[4] = swap(own, "dp", 4)
        first = swap(blocks[4][:half], "dp", 2)
        second = swap(blocks[2][half:], "dp", 4)
        blocks[6] = jnp.concatenate([first, second])
    else:
        step = 2
        while step < parts:
            for k in sorted(blocks):
                blocks[k ^ step] = swap(blocks[k], "dp", step)
            step *= 2
    for k in sorted(blocks):
        blocks[k ^ 1] = swap(blocks[k], "dp", 1)
    return jnp.concatenate([blocks[k] for k in range(parts)])


def in_order(blocks, rank, dtype):
    size = blocks[0].shape[0]
    total = jnp.zeros((size * len(blocks), blocks[0].shape[1]), dtype)
    for k, block in enumerate(blocks):
        total = lax.dynamic_update_slice(total, block.astype(dtype), ((rank ^ k) * size, 0))
    return total


def local(
    block_input,
    segments,
    positions,
    cotangent,
    gain_attn,
    w_query,
    b_query,
    w_key,
    b_key,
    w_value,
    b_value,
    w_out,
    gain_mlp,
    w_gate,
    w_up,
    w_down,
):
    bf16 = jnp.bfloat16
    f32 = jnp.float32
    dp = lax.axis_size("dp")
    tp = lax.axis_size("tensor")
    dp_rank = lax.axis_index("dp")
    tp_rank = lax.axis_index("tensor")
    row_count = block_input.shape[0]
    own_rows = row_count // tp
    width = block_input.shape[1]
    local_heads = w_query.shape[1] // HD
    score_scale = 1.0 / math.sqrt(HD)
    head_start = tp_rank * local_heads // (H // KVH) * HD
    slice_rows = width // dp

    def exchange_columns(values):
        blocks = []
        for k in range(dp):
            block = lax.dynamic_slice_in_dim(values, (dp_rank ^ k) * slice_rows, slice_rows, 1)
            blocks.append(swap(block, "dp", k) if k else block)
        return jnp.concatenate(blocks)

    def dot(a, b):
        return jnp.dot(a, b, preferred_element_type=f32)

    tokens = token_order(block_input, tp_rank, tp)
    cot = token_order(cotangent, tp_rank, tp)
    segment = token_order(segments, tp_rank, tp)
    position = token_order(positions, tp_rank, tp)
    order = token_order(jnp.arange(row_count), tp_rank, tp)

    cot_all = gather_dp(cot)

    key_own = lax.dynamic_slice_in_dim(w_key, head_start, HD, 1)
    value_own = lax.dynamic_slice_in_dim(w_value, head_start, HD, 1)
    key_bias = lax.dynamic_slice_in_dim(b_key, head_start, HD, 0)
    value_bias = lax.dynamic_slice_in_dim(b_value, head_start, HD, 0)
    input_float = tokens.astype(f32)
    rscale_attn = lax.rsqrt(jnp.mean(input_float * input_float, axis=1, keepdims=True) + eps)
    normed_attn = (input_float * rscale_attn * gain_attn).astype(bf16)
    normed_slice = exchange_columns(normed_attn)
    queries = dot(normed_attn, w_query) + b_query
    keys_pre = dot(normed_attn, key_own) + key_bias
    values_pre = dot(normed_attn, value_own) + value_bias
    cosine, sine_table = rope_tables(position)
    query_rot = rope_apply(queries.reshape(row_count, local_heads, HD), cosine, sine_table).astype(bf16)
    key_rot = rope_apply(keys_pre.reshape(row_count, 1, HD), cosine, sine_table)[:, 0].astype(bf16)
    value_heads = values_pre.astype(bf16)
    allowed = (
        (segment[:, None] == segment[None, :])
        & (order[None, :] <= order[:, None])
        & (order[None, :] // SEQ == order[:, None] // SEQ)
    )
    scores = jnp.einsum("thd,ud->htu", query_rot, key_rot, preferred_element_type=f32) * score_scale
    masked = jnp.where(allowed[None], scores, -1e30)
    row_top = jnp.max(masked, axis=2, keepdims=True)
    log_total = row_top + jnp.log(jnp.sum(jnp.exp(masked - row_top), axis=2, keepdims=True))
    probabilities = jnp.exp(masked - log_total)
    rounded_probs = probabilities.astype(bf16)
    heads_out = jnp.einsum("htu,ud->thd", rounded_probs, value_heads, preferred_element_type=f32).astype(bf16)
    heads_flat = heads_out.reshape(row_count, local_heads * HD)
    attention = reduce_blocks(dot(heads_flat, w_out), "tensor")
    heads_all = gather_dp(heads_flat)

    input_own = input_float[:own_rows]
    hidden = input_own + attention
    rscale_mlp = lax.rsqrt(jnp.mean(hidden * hidden, axis=1, keepdims=True) + eps)
    normed_own = (hidden * rscale_mlp * gain_mlp).astype(bf16)
    normed_mlp = jnp.concatenate(gather_blocks(normed_own, "tensor"))
    normed_all = gather_dp(normed_mlp)

    def mlp(normed, upstream, gate_w, up_w, down_w):
        gate_pre = dot(normed, gate_w)
        up_pre = dot(normed, up_w)
        d_act = lax.dot_general(upstream, down_w, (((1,), (1,)), ((), ())), preferred_element_type=f32)
        act_float = d_act.astype(bf16).astype(f32)
        sigmoid_gate = jax.nn.sigmoid(gate_pre)
        activated = (gate_pre * sigmoid_gate * up_pre).astype(bf16)
        d_gate = (act_float * up_pre * sigmoid_gate * (1.0 + gate_pre * (1.0 - sigmoid_gate))).astype(bf16)
        d_up = (act_float * gate_pre * sigmoid_gate).astype(bf16)
        return activated, d_gate, d_up

    activated, d_gate, d_up = mlp(normed_mlp, cot, w_gate, w_up, w_down)
    mlp_partial_grad = dot(d_gate, w_gate.T) + dot(d_up, w_up.T)
    d_normed_mlp = reduce_blocks(mlp_partial_grad, "tensor")
    grad_gain_mlp = jnp.sum(d_normed_mlp * hidden * rscale_mlp, axis=0)
    d_hidden = cot[:own_rows].astype(f32) + norm_back(hidden, rscale_mlp, gain_mlp, d_normed_mlp)
    d_hidden_b = jnp.concatenate(gather_blocks(d_hidden.astype(bf16), "tensor"))
    output_own = hidden + reduce_blocks(dot(activated, w_down), "tensor")
    output = in_order(gather_blocks(output_own.astype(bf16), "tensor"), tp_rank, f32)

    units = w_gate.shape[1] // dp
    gate_slice = lax.dynamic_slice_in_dim(w_gate, dp_rank * units, units, 1)
    up_slice = lax.dynamic_slice_in_dim(w_up, dp_rank * units, units, 1)
    down_slice = lax.dynamic_slice_in_dim(w_down, dp_rank * units, units, 0)
    activated_all, d_gate_all, d_up_all = mlp(normed_all, cot_all, gate_slice, up_slice, down_slice)
    grad_gate = dot(normed_all.T, d_gate_all).astype(bf16)
    grad_up = dot(normed_all.T, d_up_all).astype(bf16)
    grad_down = dot(activated_all.T, cot_all).astype(bf16)

    def spread(grad, row_dim):
        blocks = []
        for k in range(dp):
            block = lax.dynamic_slice_in_dim(grad, (dp_rank ^ k) * slice_rows, slice_rows, row_dim)
            blocks.append(swap(block, "dp", k) if k else block)
        return blocks

    def columns(blocks):
        total = jnp.zeros((dp,) + blocks[0].shape, bf16)
        for k, block in enumerate(blocks):
            total = lax.dynamic_update_slice(total, block[None], (dp_rank ^ k, 0, 0))
        return jnp.transpose(total, (1, 0, 2)).reshape(slice_rows, dp * units).astype(f32)

    summed_gate = columns(spread(grad_gate, 0))
    summed_up = columns(spread(grad_up, 0))
    summed_down = in_order(spread(grad_down, 1), dp_rank, f32)

    summed_out = dot(heads_all.T, exchange_columns(d_hidden_b))

    d_heads = dot(d_hidden_b, w_out.T).astype(bf16).reshape(row_count, local_heads, HD)
    d_probs = jnp.einsum("thd,ud->htu", d_heads, value_heads, preferred_element_type=f32)
    delta = jnp.sum(d_heads.astype(f32) * heads_out.astype(f32), axis=2)
    d_scores = (probabilities * (d_probs - delta.T[:, :, None]) * score_scale).astype(bf16)
    d_qrot = jnp.einsum("htu,ud->thd", d_scores, key_rot, preferred_element_type=f32)
    d_krot = jnp.einsum("htu,thd->uhd", d_scores, query_rot, preferred_element_type=f32)
    d_vhead = jnp.einsum("htu,thd->uhd", rounded_probs, d_heads, preferred_element_type=f32)
    d_query = rope_back(d_qrot, cosine, sine_table)
    d_key = rope_back(d_krot, cosine, sine_table)
    query_grad = d_query.astype(bf16).reshape(row_count, local_heads * HD)
    key_grad = jnp.sum(d_key.astype(bf16).astype(f32), axis=1).astype(bf16)
    value_grad = jnp.sum(d_vhead.astype(bf16).astype(f32), axis=1).astype(bf16)

    attn_partial_grad = dot(query_grad, w_query.T) + dot(key_grad, key_own.T) + dot(value_grad, value_own.T)
    d_normed_attn = reduce_blocks(attn_partial_grad, "tensor")
    grad_gain_attn = jnp.sum(d_normed_attn * input_own * rscale_attn[:own_rows], axis=0)
    d_input_own = d_hidden + norm_back(input_own, rscale_attn[:own_rows], gain_attn, d_normed_attn)
    d_input = in_order(gather_blocks(d_input_own.astype(bf16), "tensor"), tp_rank, f32)

    factors_all = gather_dp(jnp.concatenate([query_grad, key_grad, value_grad], axis=1))
    products = dot(normed_slice.T, factors_all)
    summed_query = products[:, : local_heads * HD]
    kv_products = products[:, local_heads * HD :]
    kv_rows = slice_rows // tp
    kv_total = [jnp.zeros((kv_rows, 2 * HD), f32) for _ in range(KVH)]
    for k in range(tp):
        block = lax.dynamic_slice_in_dim(kv_products, (tp_rank ^ k) * kv_rows, kv_rows, 0)
        block = swap(block, "tensor", k) if k else block
        source_head = (tp_rank ^ k) * local_heads // (H // KVH)
        for head in range(KVH):
            kv_total[head] = kv_total[head] + jnp.where(source_head == head, block, 0.0)
    summed_key = jnp.concatenate([total[:, :HD] for total in kv_total], axis=1)
    summed_value = jnp.concatenate([total[:, HD:] for total in kv_total], axis=1)

    bias_query = lax.dynamic_update_slice(
        jnp.zeros((H * HD,), f32),
        jnp.sum(d_query, axis=0).reshape(local_heads * HD),
        (tp_rank * local_heads * HD,),
    )
    bias_key = lax.dynamic_update_slice(
        jnp.zeros((KVH * HD,), f32), jnp.sum(d_key, axis=(0, 1)), (head_start,)
    )
    bias_value = lax.dynamic_update_slice(
        jnp.zeros((KVH * HD,), f32), jnp.sum(d_vhead, axis=(0, 1)), (head_start,)
    )
    small = jnp.concatenate([grad_gain_attn, grad_gain_mlp, bias_query, bias_key, bias_value]).reshape(-1, HD)
    for axis, size in (("dp", dp), ("tensor", tp)):
        step = 1
        while step < size:
            small = small + swap(small, axis, step)
            step *= 2
    small = small.reshape(-1)
    ends = [0, width, 2 * width, 2 * width + H * HD, 2 * width + (H + KVH) * HD, 2 * width + (H + 2 * KVH) * HD]
    gain_attn_sum, gain_mlp_sum, bias_query_sum, bias_key_sum, bias_value_sum = (
        small[a:b] for a, b in zip(ends[:-1], ends[1:])
    )
    return (
        output,
        d_input,
        gain_attn_sum,
        summed_query,
        bias_query_sum,
        summed_key,
        bias_key_sum,
        summed_value,
        bias_value_sum,
        summed_out,
        gain_mlp_sum,
        summed_gate,
        summed_up,
        summed_down,
    )


def solution(mesh):
    return jax.shard_map(
        local,
        mesh=mesh,
        in_specs=(
            P("dp", None),
            P("dp"),
            P("dp"),
            P("dp", None),
            P(),
            P(None, "tensor"),
            P("tensor"),
            P(),
            P(),
            P(),
            P(),
            P("tensor", None),
            P(),
            P(None, "tensor"),
            P(None, "tensor"),
            P("tensor", None),
        ),
        out_specs=(
            P("dp", None),
            P("dp", None),
            P(),
            P("dp", "tensor"),
            P(),
            P(("dp", "tensor"), None),
            P(),
            P(("dp", "tensor"), None),
            P(),
            P("tensor", "dp"),
            P(),
            P("dp", "tensor"),
            P("dp", "tensor"),
            P("tensor", "dp"),
        ),
        check_vma=False,
    )
```

```python
import math

import jax
import jax.numpy as jnp
from jax import lax
from jax.experimental import pallas as pl
from jax.experimental.pallas import tpu as pltpu
from jax.sharding import PartitionSpec as P

D = 1536
H = 12
KVH = 2
HD = 128
SEQ = 192


eps = 1e-06
theta = 1000000.0


def rope_tables(positions):
    exponent = jnp.arange(0, HD, 2).astype(jnp.float32) / HD
    frequency = jnp.power(jnp.float32(theta), -exponent)
    angles = positions.astype(jnp.float32)[:, None] * frequency[None, :]
    cosine = jnp.concatenate([jnp.cos(angles), jnp.cos(angles)], axis=1)
    sine_table = jnp.concatenate([jnp.sin(angles), jnp.sin(angles)], axis=1)
    return (cosine, sine_table)


def rotate(values):
    first_half = values[..., : HD // 2]
    second = values[..., HD // 2 :]
    return jnp.concatenate([-second, first_half], axis=-1)


def rope_apply(values, cosine, sine_table):
    return values * cosine[:, None, :] + rotate(values) * sine_table[:, None, :]


def rope_back(gradient, cosine, sine_table):
    return gradient * cosine[:, None, :] - rotate(gradient * sine_table[:, None, :])


def norm_back(values, rscale, gain, upstream):
    scaled = gain * upstream
    return rscale * (
        scaled - values * rscale * rscale * jnp.mean(scaled * values, axis=1, keepdims=True)
    )


def swap(values, axis, step):
    size = lax.axis_size(axis)
    return lax.ppermute(values, axis, [(rank, rank ^ step) for rank in range(size)])


def token_order(values, rank, parts):
    size = values.shape[0] // parts
    return jnp.concatenate(
        [lax.dynamic_slice_in_dim(values, (rank ^ k) * size, size, 0) for k in range(parts)]
    )


def reduce_blocks(partial, axis):
    parts = lax.axis_size(axis)
    size = partial.shape[0] // parts
    sent = partial.astype(jnp.bfloat16)
    total = partial[:size]
    for k in range(1, parts):
        total = total + swap(sent[k * size : (k + 1) * size], axis, k).astype(jnp.float32)
    return total


def gather_blocks(own, axis):
    parts = lax.axis_size(axis)
    return [own] + [swap(own, axis, k) for k in range(1, parts)]


def gather_dp(own):
    parts = lax.axis_size("dp")
    blocks = {0: own}
    if parts == 8:
        half = own.shape[0] // 2
        blocks[2] = swap(own, "dp", 2)
        blocks[4] = swap(own, "dp", 4)
        first = swap(blocks[4][:half], "dp", 2)
        second = swap(blocks[2][half:], "dp", 4)
        blocks[6] = jnp.concatenate([first, second])
    else:
        step = 2
        while step < parts:
            for k in sorted(blocks):
                blocks[k ^ step] = swap(blocks[k], "dp", step)
            step *= 2
    for k in sorted(blocks):
        blocks[k ^ 1] = swap(blocks[k], "dp", 1)
    return jnp.concatenate([blocks[k] for k in range(parts)])


def in_order(blocks, rank, dtype):
    size = blocks[0].shape[0]
    total = jnp.zeros((size * len(blocks), blocks[0].shape[1]), dtype)
    for k, block in enumerate(blocks):
        total = lax.dynamic_update_slice(total, block.astype(dtype), ((rank ^ k) * size, 0))
    return total


def place_kernel(rank, *refs):
    parts = len(refs) - 4
    pieces, (gate_out, up_out, down_out, buffer) = refs[:parts], refs[parts:]
    units = pieces[0].shape[2]
    for k in range(parts):
        buffer[rank[0] ^ k] = pieces[k][...]
    for j in range(parts):
        gate_out[:, j * units : (j + 1) * units] = buffer[j, 0].astype(jnp.float32)
        up_out[:, j * units : (j + 1) * units] = buffer[j, 1].astype(jnp.float32)
        down_out[j * units : (j + 1) * units, :] = buffer[j, 2].astype(jnp.float32).T


def place(pieces, rank):
    parts = len(pieces)
    _, rows, units = pieces[0].shape
    wide = jax.ShapeDtypeStruct((rows, parts * units), jnp.float32)
    tall = jax.ShapeDtypeStruct((parts * units, rows), jnp.float32)
    vmem = pl.BlockSpec(memory_space=pltpu.VMEM)
    return pl.pallas_call(
        place_kernel,
        out_shape=(wide, wide, tall),
        in_specs=[pl.BlockSpec(memory_space=pltpu.SMEM)] + [vmem] * parts,
        out_specs=(vmem, vmem, vmem),
        scratch_shapes=[pltpu.VMEM((parts,) + pieces[0].shape, jnp.bfloat16)],
        name="place",
    )(rank.reshape(1), *pieces)


def local(
    block_input,
    segments,
    positions,
    cotangent,
    gain_attn,
    w_query,
    b_query,
    w_key,
    b_key,
    w_value,
    b_value,
    w_out,
    gain_mlp,
    w_gate,
    w_up,
    w_down,
):
    bf16 = jnp.bfloat16
    f32 = jnp.float32
    dp = lax.axis_size("dp")
    tp = lax.axis_size("tensor")
    dp_rank = lax.axis_index("dp")
    tp_rank = lax.axis_index("tensor")
    row_count = block_input.shape[0]
    own_rows = row_count // tp
    width = block_input.shape[1]
    local_heads = w_query.shape[1] // HD
    score_scale = 1.0 / math.sqrt(HD)
    head_start = tp_rank * local_heads // (H // KVH) * HD
    slice_rows = width // dp

    def exchange_columns(values):
        blocks = []
        for k in range(dp):
            block = lax.dynamic_slice_in_dim(values, (dp_rank ^ k) * slice_rows, slice_rows, 1)
            blocks.append(swap(block, "dp", k) if k else block)
        return jnp.concatenate(blocks)

    def dot(a, b):
        return jnp.dot(a, b, preferred_element_type=f32)

    tokens = token_order(block_input, tp_rank, tp)
    cot = token_order(cotangent, tp_rank, tp)
    segment = token_order(segments, tp_rank, tp)
    position = token_order(positions, tp_rank, tp)
    order = token_order(jnp.arange(row_count), tp_rank, tp)

    cot_all = gather_dp(cot)

    key_own = lax.dynamic_slice_in_dim(w_key, head_start, HD, 1)
    value_own = lax.dynamic_slice_in_dim(w_value, head_start, HD, 1)
    key_bias = lax.dynamic_slice_in_dim(b_key, head_start, HD, 0)
    value_bias = lax.dynamic_slice_in_dim(b_value, head_start, HD, 0)
    input_float = tokens.astype(f32)
    rscale_attn = lax.rsqrt(jnp.mean(input_float * input_float, axis=1, keepdims=True) + eps)
    normed_attn = (input_float * rscale_attn * gain_attn).astype(bf16)
    normed_slice = exchange_columns(normed_attn)
    queries = dot(normed_attn, w_query) + b_query
    keys_pre = dot(normed_attn, key_own) + key_bias
    values_pre = dot(normed_attn, value_own) + value_bias
    cosine, sine_table = rope_tables(position)
    query_rot = rope_apply(queries.reshape(row_count, local_heads, HD), cosine, sine_table).astype(bf16)
    key_rot = rope_apply(keys_pre.reshape(row_count, 1, HD), cosine, sine_table)[:, 0].astype(bf16)
    value_heads = values_pre.astype(bf16)
    allowed = (
        (segment[:, None] == segment[None, :])
        & (order[None, :] <= order[:, None])
        & (order[None, :] // SEQ == order[:, None] // SEQ)
    )
    scores = jnp.einsum("thd,ud->htu", query_rot, key_rot, preferred_element_type=f32) * score_scale
    masked = jnp.where(allowed[None], scores, -1e30)
    row_top = jnp.max(masked, axis=2, keepdims=True)
    log_total = row_top + jnp.log(jnp.sum(jnp.exp(masked - row_top), axis=2, keepdims=True))
    probabilities = jnp.exp(masked - log_total)
    rounded_probs = probabilities.astype(bf16)
    heads_out = jnp.einsum("htu,ud->thd", rounded_probs, value_heads, preferred_element_type=f32).astype(bf16)
    heads_flat = heads_out.reshape(row_count, local_heads * HD)
    attention = reduce_blocks(dot(heads_flat, w_out), "tensor")
    heads_all = gather_dp(heads_flat)

    input_own = input_float[:own_rows]
    hidden = input_own + attention
    rscale_mlp = lax.rsqrt(jnp.mean(hidden * hidden, axis=1, keepdims=True) + eps)
    normed_own = (hidden * rscale_mlp * gain_mlp).astype(bf16)
    normed_mlp = jnp.concatenate(gather_blocks(normed_own, "tensor"))
    normed_all = gather_dp(normed_mlp)

    def mlp(normed, upstream, gate_w, up_w, down_w):
        gate_pre = dot(normed, gate_w)
        up_pre = dot(normed, up_w)
        d_act = lax.dot_general(upstream, down_w, (((1,), (1,)), ((), ())), preferred_element_type=f32)
        act_float = d_act.astype(bf16).astype(f32)
        sigmoid_gate = jax.nn.sigmoid(gate_pre)
        activated = (gate_pre * sigmoid_gate * up_pre).astype(bf16)
        d_gate = (act_float * up_pre * sigmoid_gate * (1.0 + gate_pre * (1.0 - sigmoid_gate))).astype(bf16)
        d_up = (act_float * gate_pre * sigmoid_gate).astype(bf16)
        return activated, d_gate, d_up

    activated, d_gate, d_up = mlp(normed_mlp, cot, w_gate, w_up, w_down)
    mlp_partial_grad = dot(d_gate, w_gate.T) + dot(d_up, w_up.T)
    d_normed_mlp = reduce_blocks(mlp_partial_grad, "tensor")
    grad_gain_mlp = jnp.sum(d_normed_mlp * hidden * rscale_mlp, axis=0)
    d_hidden = cot[:own_rows].astype(f32) + norm_back(hidden, rscale_mlp, gain_mlp, d_normed_mlp)
    d_hidden_b = jnp.concatenate(gather_blocks(d_hidden.astype(bf16), "tensor"))
    output_own = hidden + reduce_blocks(dot(activated, w_down), "tensor")
    output = in_order(gather_blocks(output_own.astype(bf16), "tensor"), tp_rank, f32)

    units = w_gate.shape[1] // dp
    gate_slice = lax.dynamic_slice_in_dim(w_gate, dp_rank * units, units, 1)
    up_slice = lax.dynamic_slice_in_dim(w_up, dp_rank * units, units, 1)
    down_slice = lax.dynamic_slice_in_dim(w_down, dp_rank * units, units, 0)
    activated_all, d_gate_all, d_up_all = mlp(normed_all, cot_all, gate_slice, up_slice, down_slice)
    grads = [dot(normed_all.T, d_gate_all), dot(normed_all.T, d_up_all), dot(cot_all.T, activated_all)]
    grads = jnp.stack([grad.astype(bf16) for grad in grads])
    pieces = []
    for k in range(dp):
        piece = lax.dynamic_slice_in_dim(grads, (dp_rank ^ k) * slice_rows, slice_rows, 1)
        pieces.append(swap(piece, "dp", k) if k else piece)
    summed_gate, summed_up, summed_down = place(pieces, dp_rank)

    summed_out = dot(heads_all.T, exchange_columns(d_hidden_b))

    d_heads = dot(d_hidden_b, w_out.T).astype(bf16).reshape(row_count, local_heads, HD)
    d_probs = jnp.einsum("thd,ud->htu", d_heads, value_heads, preferred_element_type=f32)
    delta = jnp.sum(d_heads.astype(f32) * heads_out.astype(f32), axis=2)
    d_scores = (probabilities * (d_probs - delta.T[:, :, None]) * score_scale).astype(bf16)
    d_qrot = jnp.einsum("htu,ud->thd", d_scores, key_rot, preferred_element_type=f32)
    d_krot = jnp.einsum("htu,thd->uhd", d_scores, query_rot, preferred_element_type=f32)
    d_vhead = jnp.einsum("htu,thd->uhd", rounded_probs, d_heads, preferred_element_type=f32)
    d_query = rope_back(d_qrot, cosine, sine_table)
    d_key = rope_back(d_krot, cosine, sine_table)
    query_grad = d_query.astype(bf16).reshape(row_count, local_heads * HD)
    key_grad = jnp.sum(d_key.astype(bf16).astype(f32), axis=1).astype(bf16)
    value_grad = jnp.sum(d_vhead.astype(bf16).astype(f32), axis=1).astype(bf16)

    attn_partial_grad = dot(query_grad, w_query.T) + dot(key_grad, key_own.T) + dot(value_grad, value_own.T)
    d_normed_attn = reduce_blocks(attn_partial_grad, "tensor")
    grad_gain_attn = jnp.sum(d_normed_attn * input_own * rscale_attn[:own_rows], axis=0)
    d_input_own = d_hidden + norm_back(input_own, rscale_attn[:own_rows], gain_attn, d_normed_attn)
    d_input = in_order(gather_blocks(d_input_own.astype(bf16), "tensor"), tp_rank, f32)

    factors_all = gather_dp(jnp.concatenate([query_grad, key_grad, value_grad], axis=1))
    products = dot(normed_slice.T, factors_all)
    summed_query = products[:, : local_heads * HD]
    kv_products = products[:, local_heads * HD :]
    kv_rows = slice_rows // tp
    kv_total = [jnp.zeros((kv_rows, 2 * HD), f32) for _ in range(KVH)]
    for k in range(tp):
        block = lax.dynamic_slice_in_dim(kv_products, (tp_rank ^ k) * kv_rows, kv_rows, 0)
        block = swap(block, "tensor", k) if k else block
        source_head = (tp_rank ^ k) * local_heads // (H // KVH)
        for head in range(KVH):
            kv_total[head] = kv_total[head] + jnp.where(source_head == head, block, 0.0)
    summed_key = jnp.concatenate([total[:, :HD] for total in kv_total], axis=1)
    summed_value = jnp.concatenate([total[:, HD:] for total in kv_total], axis=1)

    bias_query = lax.dynamic_update_slice(
        jnp.zeros((H * HD,), f32),
        jnp.sum(d_query, axis=0).reshape(local_heads * HD),
        (tp_rank * local_heads * HD,),
    )
    bias_key = lax.dynamic_update_slice(
        jnp.zeros((KVH * HD,), f32), jnp.sum(d_key, axis=(0, 1)), (head_start,)
    )
    bias_value = lax.dynamic_update_slice(
        jnp.zeros((KVH * HD,), f32), jnp.sum(d_vhead, axis=(0, 1)), (head_start,)
    )
    small = jnp.concatenate([grad_gain_attn, grad_gain_mlp, bias_query, bias_key, bias_value]).reshape(-1, HD)
    for axis, size in (("dp", dp), ("tensor", tp)):
        step = 1
        while step < size:
            small = small + swap(small, axis, step)
            step *= 2
    small = small.reshape(-1)
    ends = [0, width, 2 * width, 2 * width + H * HD, 2 * width + (H + KVH) * HD, 2 * width + (H + 2 * KVH) * HD]
    gain_attn_sum, gain_mlp_sum, bias_query_sum, bias_key_sum, bias_value_sum = (
        small[a:b] for a, b in zip(ends[:-1], ends[1:])
    )
    return (
        output,
        d_input,
        gain_attn_sum,
        summed_query,
        bias_query_sum,
        summed_key,
        bias_key_sum,
        summed_value,
        bias_value_sum,
        summed_out,
        gain_mlp_sum,
        summed_gate,
        summed_up,
        summed_down,
    )


def solution(mesh):
    return jax.shard_map(
        local,
        mesh=mesh,
        in_specs=(
            P("dp", None),
            P("dp"),
            P("dp"),
            P("dp", None),
            P(),
            P(None, "tensor"),
            P("tensor"),
            P(),
            P(),
            P(),
            P(),
            P("tensor", None),
            P(),
            P(None, "tensor"),
            P(None, "tensor"),
            P("tensor", None),
        ),
        out_specs=(
            P("dp", None),
            P("dp", None),
            P(),
            P("dp", "tensor"),
            P(),
            P(("dp", "tensor"), None),
            P(),
            P(("dp", "tensor"), None),
            P(),
            P("tensor", "dp"),
            P(),
            P("dp", "tensor"),
            P("dp", "tensor"),
            P("tensor", "dp"),
        ),
        check_vma=False,
    )
```

```python
import functools
import math

import jax
import jax.numpy as jnp
from jax import lax
from jax.experimental import pallas as pl
from jax.experimental.pallas import tpu as pltpu
from jax.sharding import PartitionSpec as P

D = 1536
H = 12
KVH = 2
HD = 128
SEQ = 192


eps = 1e-06
theta = 1000000.0


def rope_tables(positions):
    exponent = jnp.arange(0, HD, 2).astype(jnp.float32) / HD
    frequency = jnp.power(jnp.float32(theta), -exponent)
    angles = positions.astype(jnp.float32)[:, None] * frequency[None, :]
    cosine = jnp.concatenate([jnp.cos(angles), jnp.cos(angles)], axis=1)
    sine_table = jnp.concatenate([jnp.sin(angles), jnp.sin(angles)], axis=1)
    return (cosine, sine_table)


def rotate(values):
    first_half = values[..., : HD // 2]
    second = values[..., HD // 2 :]
    return jnp.concatenate([-second, first_half], axis=-1)


def rope_apply(values, cosine, sine_table):
    return values * cosine[:, None, :] + rotate(values) * sine_table[:, None, :]


def rope_back(gradient, cosine, sine_table):
    return gradient * cosine[:, None, :] - rotate(gradient * sine_table[:, None, :])


def norm_back(values, rscale, gain, upstream):
    scaled = gain * upstream
    return rscale * (
        scaled - values * rscale * rscale * jnp.mean(scaled * values, axis=1, keepdims=True)
    )


def swap(values, axis, step):
    size = lax.axis_size(axis)
    return lax.ppermute(values, axis, [(rank, rank ^ step) for rank in range(size)])


def gather_dp(own):
    parts = lax.axis_size("dp")
    if parts == 8:
        half = own.shape[0] // 2
        along_x = swap(own, "dp", 2)
        along_y = swap(own, "dp", 4)
        chips = [own, along_x, along_y, swap(along_y[:half], "dp", 2), swap(along_x[half:], "dp", 4)]
    else:
        chips = [own]
        step = 2
        while step < parts:
            chips = chips + [swap(chip, "dp", step) for chip in chips]
            step *= 2
    return chips + [swap(chip, "dp", 1) for chip in chips]


VMEM = pl.BlockSpec(memory_space=pltpu.VMEM)
SMEM = pl.BlockSpec(memory_space=pltpu.SMEM)
ANY = pl.BlockSpec(memory_space=pl.ANY)


def arrange_kernel(rank, *refs):
    blocks, out = refs[:-1], refs[-1]
    size = blocks[0].shape[0]
    for k, block in enumerate(blocks):
        start = pl.multiple_of((rank[0] ^ k) * size, size)
        out[pl.ds(start, size), :] = block[...].astype(out.dtype)


def arrange(own, axis, rank, dtype):
    parts = lax.axis_size(axis)
    blocks = [own] + [swap(own, axis, k) for k in range(1, parts)]
    size, width = own.shape
    return pl.pallas_call(
        arrange_kernel,
        out_shape=jax.ShapeDtypeStruct((parts * size, width), dtype),
        in_specs=[SMEM] + [VMEM] * parts,
        out_specs=VMEM,
        name="arrange",
    )(rank.reshape(1), *blocks)


def fetch(sources, target, sems, first):
    copies = []
    row = 0
    for k, source in enumerate(sources):
        rows = source.shape[0]
        copy = pltpu.make_async_copy(source, target.at[pl.ds(row, rows)], sems.at[first + k])
        copy.start()
        copies.append(copy)
        row += rows
    return copies


def product(a, b, dims):
    return lax.dot_general(a, b, (dims, ((), ())), preferred_element_type=jnp.float32)


def slice_kernel(count, parts, rank, *refs):
    normed_refs, cot_refs = refs[:count], refs[count : 2 * count]
    gate_up, down = refs[2 * count : 2 * count + 2]
    outs = refs[2 * count + 2 : 2 * count + 2 + parts]
    normed, cot, wide, narrow, pieces, sems = refs[2 * count + 2 + parts :]
    padded = down.shape[0]
    tokens, width = normed.shape
    _, units, rows = outs[0].shape
    f32, bf16 = jnp.float32, jnp.bfloat16
    waits = fetch(normed_refs, normed, sems, 0) + fetch(cot_refs, cot, sems, count)
    for copy in waits:
        copy.wait()
    chunk = 256

    def forward(step, carry):
        at = pl.ds(pl.multiple_of(step * chunk, chunk), chunk)
        pre = product(gate_up[...], normed[at, :], ((1,), (1,)))
        act = product(down[...], cot[at, :], ((1,), (1,))).astype(bf16).astype(f32)
        gate, up = pre[:padded], pre[padded:]
        sigmoid = jax.nn.sigmoid(gate)
        wide[:padded, at] = (act * up * sigmoid * (1.0 + gate * (1.0 - sigmoid))).astype(bf16)
        wide[padded:, at] = (act * gate * sigmoid).astype(bf16)
        narrow[:, at] = (gate * sigmoid * up).astype(bf16)
        return carry

    lax.fori_loop(0, tokens // chunk, forward, 0)
    block = 2 * rows if (2 * rows) % 128 == 0 else width
    per = block // rows

    def backward(step, carry):
        at = pl.ds(pl.multiple_of(step * block, block), block)
        both = product(wide[...], normed[:, at], ((1,), (0,))).astype(bf16)
        last = product(narrow[...], cot[:, at], ((1,), (0,))).astype(bf16)
        for k in range(per):
            cols = slice(k * rows, (k + 1) * rows)
            pieces[step * per + k, 0] = both[:units, cols]
            pieces[step * per + k, 1] = both[padded : padded + units, cols]
            pieces[step * per + k, 2] = last[:units, cols]
        return carry

    lax.fori_loop(0, width // block, backward, 0)
    for k in range(parts):
        outs[k][...] = pieces[rank[0] ^ k]


def slice_grads(normed_blocks, cot_blocks, gate_up, down, rank, parts, units):
    count = len(normed_blocks)
    padded, width = down.shape
    tokens = sum(block.shape[0] for block in normed_blocks)
    rows = width // parts
    bf16 = jnp.bfloat16
    return pl.pallas_call(
        functools.partial(slice_kernel, count, parts),
        out_shape=[jax.ShapeDtypeStruct((3, units, rows), bf16)] * parts,
        in_specs=[SMEM] + [ANY] * (2 * count) + [VMEM, VMEM],
        out_specs=[VMEM] * parts,
        scratch_shapes=[
            pltpu.VMEM((tokens, width), bf16),
            pltpu.VMEM((tokens, width), bf16),
            pltpu.VMEM((2 * padded, tokens), bf16),
            pltpu.VMEM((padded, tokens), bf16),
            pltpu.VMEM((parts, 3, units, rows), bf16),
            pltpu.SemaphoreType.DMA((2 * count,)),
        ],
        name="slice_grads",
    )(rank.reshape(1), *normed_blocks, *cot_blocks, gate_up, down)


def place_kernel(rank, *refs):
    parts = len(refs) - 4
    pieces, (gate_out, up_out, down_out, buffer) = refs[:parts], refs[parts:]
    units = pieces[0].shape[1]
    for k in range(parts):
        buffer[rank[0] ^ k] = pieces[k][...]
    for j in range(parts):
        gate_out[:, j * units : (j + 1) * units] = buffer[j, 0].astype(jnp.float32).T
        up_out[:, j * units : (j + 1) * units] = buffer[j, 1].astype(jnp.float32).T
        down_out[j * units : (j + 1) * units, :] = buffer[j, 2].astype(jnp.float32)


def place(pieces, rank):
    parts = len(pieces)
    _, units, rows = pieces[0].shape
    wide = jax.ShapeDtypeStruct((rows, parts * units), jnp.float32)
    tall = jax.ShapeDtypeStruct((parts * units, rows), jnp.float32)
    return pl.pallas_call(
        place_kernel,
        out_shape=(wide, wide, tall),
        in_specs=[SMEM] + [VMEM] * parts,
        out_specs=(VMEM, VMEM, VMEM),
        scratch_shapes=[pltpu.VMEM((parts,) + pieces[0].shape, jnp.bfloat16)],
        name="place",
    )(rank.reshape(1), *pieces)


def outer_kernel(left_count, right_count, *refs):
    left_refs = refs[:left_count]
    right_refs = refs[left_count : left_count + right_count]
    out, left, right, sems = refs[left_count + right_count :]
    waits = fetch(left_refs, left, sems, 0) + fetch(right_refs, right, sems, left_count)
    for copy in waits:
        copy.wait()
    out[...] = product(left[...], right[...], ((0,), (0,)))


def outer(left_blocks, right_blocks):
    tokens = sum(block.shape[0] for block in left_blocks)
    left_width, right_width = left_blocks[0].shape[1], right_blocks[0].shape[1]
    counts = (len(left_blocks), len(right_blocks))
    return pl.pallas_call(
        functools.partial(outer_kernel, *counts),
        out_shape=jax.ShapeDtypeStruct((left_width, right_width), jnp.float32),
        in_specs=[ANY] * sum(counts),
        out_specs=VMEM,
        scratch_shapes=[
            pltpu.VMEM((tokens, left_width), jnp.bfloat16),
            pltpu.VMEM((tokens, right_width), jnp.bfloat16),
            pltpu.SemaphoreType.DMA((sum(counts),)),
        ],
        name="outer",
    )(*left_blocks, *right_blocks)


def local(
    block_input,
    segments,
    positions,
    cotangent,
    gain_attn,
    w_query,
    b_query,
    w_key,
    b_key,
    w_value,
    b_value,
    w_out,
    gain_mlp,
    w_gate,
    w_up,
    w_down,
):
    bf16 = jnp.bfloat16
    f32 = jnp.float32
    dp = lax.axis_size("dp")
    tp = lax.axis_size("tensor")
    dp_rank = lax.axis_index("dp")
    tp_rank = lax.axis_index("tensor")
    row_count = block_input.shape[0]
    own_rows = row_count // tp
    width = block_input.shape[1]
    local_heads = w_query.shape[1] // HD
    score_scale = 1.0 / math.sqrt(HD)
    head_start = tp_rank * local_heads // (H // KVH) * HD
    slice_rows = width // dp

    def exchange_columns(values):
        blocks = []
        for k in [*range(0, dp, 2), *range(1, dp, 2)]:
            block = lax.dynamic_slice_in_dim(values, (dp_rank ^ k) * slice_rows, slice_rows, 1)
            blocks.append(swap(block, "dp", k) if k else block)
        return blocks

    def dot(a, b):
        return jnp.dot(a, b, preferred_element_type=f32)

    def own_block(values):
        return lax.dynamic_slice_in_dim(values, tp_rank * own_rows, own_rows, 0)

    def reduce_tensor(partial):
        sent = partial.astype(bf16)
        total = own_block(partial)
        for k in range(1, tp):
            block = lax.dynamic_slice_in_dim(sent, (tp_rank ^ k) * own_rows, own_rows, 0)
            total = total + swap(block, "tensor", k).astype(f32)
        return total

    units = w_gate.shape[1] // dp
    padding = ((0, -units % 16), (0, 0))
    gate_slice = lax.dynamic_slice_in_dim(w_gate, dp_rank * units, units, 1).T
    up_slice = lax.dynamic_slice_in_dim(w_up, dp_rank * units, units, 1).T
    down_slice = lax.dynamic_slice_in_dim(w_down, dp_rank * units, units, 0)
    gate_up = jnp.concatenate([jnp.pad(gate_slice, padding), jnp.pad(up_slice, padding)])
    down_slice = jnp.pad(down_slice, padding)

    tokens = block_input
    cot = cotangent
    cot_blocks = gather_dp(cot)

    key_own = lax.dynamic_slice_in_dim(w_key, head_start, HD, 1)
    value_own = lax.dynamic_slice_in_dim(w_value, head_start, HD, 1)
    key_bias = lax.dynamic_slice_in_dim(b_key, head_start, HD, 0)
    value_bias = lax.dynamic_slice_in_dim(b_value, head_start, HD, 0)
    input_float = tokens.astype(f32)
    rscale_attn = lax.rsqrt(jnp.mean(input_float * input_float, axis=1, keepdims=True) + eps)
    normed_attn = (input_float * rscale_attn * gain_attn).astype(bf16)
    normed_slice = exchange_columns(normed_attn)
    queries = dot(normed_attn, w_query) + b_query
    keys_pre = dot(normed_attn, key_own) + key_bias
    values_pre = dot(normed_attn, value_own) + value_bias
    cosine, sine_table = rope_tables(positions)
    query_rot = rope_apply(queries.reshape(row_count, local_heads, HD), cosine, sine_table).astype(bf16)
    key_rot = rope_apply(keys_pre.reshape(row_count, 1, HD), cosine, sine_table)[:, 0].astype(bf16)
    value_heads = values_pre.astype(bf16)
    order = jnp.arange(row_count)
    allowed = (
        (segments[:, None] == segments[None, :])
        & (order[None, :] <= order[:, None])
        & (order[None, :] // SEQ == order[:, None] // SEQ)
    )
    scores = jnp.einsum("thd,ud->htu", query_rot, key_rot, preferred_element_type=f32) * score_scale
    masked = jnp.where(allowed[None], scores, -1e30)
    row_top = jnp.max(masked, axis=2, keepdims=True)
    log_total = row_top + jnp.log(jnp.sum(jnp.exp(masked - row_top), axis=2, keepdims=True))
    probabilities = jnp.exp(masked - log_total)
    rounded_probs = probabilities.astype(bf16)
    heads_out = jnp.einsum("htu,ud->thd", rounded_probs, value_heads, preferred_element_type=f32).astype(bf16)
    heads_flat = heads_out.reshape(row_count, local_heads * HD)
    attention = reduce_tensor(dot(heads_flat, w_out))
    heads_blocks = gather_dp(heads_flat)

    input_own = own_block(input_float)
    rscale_own = own_block(rscale_attn)
    hidden = input_own + attention
    rscale_mlp = lax.rsqrt(jnp.mean(hidden * hidden, axis=1, keepdims=True) + eps)
    normed_mlp = arrange((hidden * rscale_mlp * gain_mlp).astype(bf16), "tensor", tp_rank, bf16)
    normed_blocks = gather_dp(normed_mlp)

    def mlp(normed, upstream, gate_w, up_w, down_w):
        gate_pre = dot(normed, gate_w)
        up_pre = dot(normed, up_w)
        d_act = lax.dot_general(upstream, down_w, (((1,), (1,)), ((), ())), preferred_element_type=f32)
        act_float = d_act.astype(bf16).astype(f32)
        sigmoid_gate = jax.nn.sigmoid(gate_pre)
        activated = (gate_pre * sigmoid_gate * up_pre).astype(bf16)
        d_gate = (act_float * up_pre * sigmoid_gate * (1.0 + gate_pre * (1.0 - sigmoid_gate))).astype(bf16)
        d_up = (act_float * gate_pre * sigmoid_gate).astype(bf16)
        return activated, d_gate, d_up

    activated, d_gate, d_up = mlp(normed_mlp, cot, w_gate, w_up, w_down)
    mlp_partial_grad = dot(d_gate, w_gate.T) + dot(d_up, w_up.T)
    d_normed_mlp = reduce_tensor(mlp_partial_grad)
    grad_gain_mlp = jnp.sum(d_normed_mlp * hidden * rscale_mlp, axis=0)
    d_hidden = own_block(cot).astype(f32) + norm_back(hidden, rscale_mlp, gain_mlp, d_normed_mlp)
    d_hidden_b = arrange(d_hidden.astype(bf16), "tensor", tp_rank, bf16)
    output_own = hidden + reduce_tensor(dot(activated, w_down))
    output = arrange(output_own.astype(bf16), "tensor", tp_rank, f32)

    pieces = slice_grads(normed_blocks, cot_blocks, gate_up, down_slice, dp_rank, dp, units)
    pieces = [swap(piece, "dp", k) if k else piece for k, piece in enumerate(pieces)]
    summed_gate, summed_up, summed_down = place(pieces, dp_rank)
    summed_out = outer(heads_blocks, exchange_columns(d_hidden_b))

    d_heads = dot(d_hidden_b, w_out.T).astype(bf16).reshape(row_count, local_heads, HD)
    d_probs = jnp.einsum("thd,ud->htu", d_heads, value_heads, preferred_element_type=f32)
    delta = jnp.sum(d_heads.astype(f32) * heads_out.astype(f32), axis=2)
    d_scores = (probabilities * (d_probs - delta.T[:, :, None]) * score_scale).astype(bf16)
    d_qrot = jnp.einsum("htu,ud->thd", d_scores, key_rot, preferred_element_type=f32)
    d_krot = jnp.einsum("htu,thd->uhd", d_scores, query_rot, preferred_element_type=f32)
    d_vhead = jnp.einsum("htu,thd->uhd", rounded_probs, d_heads, preferred_element_type=f32)
    d_query = rope_back(d_qrot, cosine, sine_table)
    d_key = rope_back(d_krot, cosine, sine_table)
    query_grad = d_query.astype(bf16).reshape(row_count, local_heads * HD)
    key_grad = jnp.sum(d_key.astype(bf16).astype(f32), axis=1).astype(bf16)
    value_grad = jnp.sum(d_vhead.astype(bf16).astype(f32), axis=1).astype(bf16)

    attn_partial_grad = dot(query_grad, w_query.T) + dot(key_grad, key_own.T) + dot(value_grad, value_own.T)
    d_normed_attn = reduce_tensor(attn_partial_grad)
    grad_gain_attn = jnp.sum(d_normed_attn * input_own * rscale_own, axis=0)
    d_input_own = d_hidden + norm_back(input_own, rscale_own, gain_attn, d_normed_attn)
    d_input = arrange(d_input_own.astype(bf16), "tensor", tp_rank, f32)

    factor_blocks = gather_dp(jnp.concatenate([query_grad, key_grad, value_grad], axis=1))
    products = outer(normed_slice, factor_blocks)
    summed_query = products[:, : local_heads * HD]
    kv_products = products[:, local_heads * HD :]
    kv_rows = slice_rows // tp
    kv_total = [jnp.zeros((kv_rows, 2 * HD), f32) for _ in range(KVH)]
    for k in range(tp):
        block = lax.dynamic_slice_in_dim(kv_products, (tp_rank ^ k) * kv_rows, kv_rows, 0)
        block = swap(block, "tensor", k) if k else block
        source_head = (tp_rank ^ k) * local_heads // (H // KVH)
        for head in range(KVH):
            kv_total[head] = kv_total[head] + jnp.where(source_head == head, block, 0.0)
    summed_key = jnp.concatenate([total[:, :HD] for total in kv_total], axis=1)
    summed_value = jnp.concatenate([total[:, HD:] for total in kv_total], axis=1)

    bias_query = lax.dynamic_update_slice(
        jnp.zeros((H * HD,), f32),
        jnp.sum(d_query, axis=0).reshape(local_heads * HD),
        (tp_rank * local_heads * HD,),
    )
    bias_key = lax.dynamic_update_slice(
        jnp.zeros((KVH * HD,), f32), jnp.sum(d_key, axis=(0, 1)), (head_start,)
    )
    bias_value = lax.dynamic_update_slice(
        jnp.zeros((KVH * HD,), f32), jnp.sum(d_vhead, axis=(0, 1)), (head_start,)
    )
    small = jnp.concatenate([grad_gain_attn, grad_gain_mlp, bias_query, bias_key, bias_value]).reshape(-1, HD)
    for axis, size in (("dp", dp), ("tensor", tp)):
        step = 1
        while step < size:
            small = small + swap(small, axis, step)
            step *= 2
    small = small.reshape(-1)
    ends = [0, width, 2 * width, 2 * width + H * HD, 2 * width + (H + KVH) * HD, 2 * width + (H + 2 * KVH) * HD]
    gain_attn_sum, gain_mlp_sum, bias_query_sum, bias_key_sum, bias_value_sum = (
        small[a:b] for a, b in zip(ends[:-1], ends[1:])
    )
    return (
        output,
        d_input,
        gain_attn_sum,
        summed_query,
        bias_query_sum,
        summed_key,
        bias_key_sum,
        summed_value,
        bias_value_sum,
        summed_out,
        gain_mlp_sum,
        summed_gate,
        summed_up,
        summed_down,
    )


def solution(mesh):
    return jax.shard_map(
        local,
        mesh=mesh,
        in_specs=(
            P("dp", None),
            P("dp"),
            P("dp"),
            P("dp", None),
            P(),
            P(None, "tensor"),
            P("tensor"),
            P(),
            P(),
            P(),
            P(),
            P("tensor", None),
            P(),
            P(None, "tensor"),
            P(None, "tensor"),
            P("tensor", None),
        ),
        out_specs=(
            P("dp", None),
            P("dp", None),
            P(),
            P("dp", "tensor"),
            P(),
            P(("dp", "tensor"), None),
            P(),
            P(("dp", "tensor"), None),
            P(),
            P("tensor", "dp"),
            P(),
            P("dp", "tensor"),
            P("dp", "tensor"),
            P("tensor", "dp"),
        ),
        check_vma=False,
    )
```

```python
import functools
import math

import jax
import jax.numpy as jnp
from jax import lax
from jax.experimental import pallas as pl
from jax.experimental.pallas import tpu as pltpu
from jax.sharding import PartitionSpec as P


H = 12
KVH = 2
HD = 128
SEQ = 192


eps = 1e-06
theta = 1000000.0


def rope_tables(positions):
    exponent = jnp.arange(0, HD, 2).astype(jnp.float32) / HD
    frequency = jnp.power(jnp.float32(theta), -exponent)
    angles = positions.astype(jnp.float32)[:, None] * frequency[None, :]
    cosine = jnp.concatenate([jnp.cos(angles), jnp.cos(angles)], axis=1)
    sine_table = jnp.concatenate([jnp.sin(angles), jnp.sin(angles)], axis=1)
    return (cosine, sine_table)


def rotate(values):
    first_half = values[..., : HD // 2]
    second = values[..., HD // 2 :]
    return jnp.concatenate([-second, first_half], axis=-1)


def rope_apply(values, cosine, sine_table):
    return values * cosine[:, None, :] + rotate(values) * sine_table[:, None, :]


def rope_back(gradient, cosine, sine_table):
    return gradient * cosine[:, None, :] - rotate(gradient * sine_table[:, None, :])


def norm_back(values, rscale, gain, upstream):
    scaled = gain * upstream
    return rscale * (
        scaled - values * rscale * rscale * jnp.mean(scaled * values, axis=1, keepdims=True)
    )


def swap(values, axis, step):
    size = lax.axis_size(axis)
    return lax.ppermute(values, axis, [(rank, rank ^ step) for rank in range(size)])


def gather_dp(own):
    parts = lax.axis_size("dp")
    near, far = [own], []
    if parts == 8:
        half = own.shape[0] // 2
        along_x = swap(own, "dp", 2)
        along_y = swap(own, "dp", 4)
        near = [own, along_x, along_y]
        far = [swap(along_y[:half], "dp", 2), swap(along_x[half:], "dp", 4)]
    else:
        step = 2
        while step < parts:
            near = near + [swap(chip, "dp", step) for chip in near]
            step *= 2
    partner = [swap(chip, "dp", 1) for chip in near]
    partner += [swap(chip, "dp", 1) for chip in far]
    return near + far + partner


VMEM = pl.BlockSpec(memory_space=pltpu.VMEM)
SMEM = pl.BlockSpec(memory_space=pltpu.SMEM)
ANY = pl.BlockSpec(memory_space=pl.ANY)


def arrange_kernel(rank, *refs):
    blocks, out = refs[:-1], refs[-1]
    size = blocks[0].shape[0]
    for k, block in enumerate(blocks):
        start = pl.multiple_of((rank[0] ^ k) * size, size)
        out[pl.ds(start, size), :] = block[...].astype(out.dtype)


def arrange(own, axis, rank, dtype):
    parts = lax.axis_size(axis)
    blocks = [own] + [swap(own, axis, k) for k in range(1, parts)]
    size, width = own.shape
    return pl.pallas_call(
        arrange_kernel,
        out_shape=jax.ShapeDtypeStruct((parts * size, width), dtype),
        in_specs=[SMEM] + [VMEM] * parts,
        out_specs=VMEM,
        name="arrange",
    )(rank.reshape(1), *blocks)


def fetch(sources, target, sems, first):
    copies = []
    row = 0
    for k, source in enumerate(sources):
        rows = source.shape[0]
        copy = pltpu.make_async_copy(source, target.at[pl.ds(row, rows)], sems.at[first + k])
        copy.start()
        copies.append(copy)
        row += rows
    return copies


def product(a, b, dims):
    return lax.dot_general(a, b, (dims, ((), ())), preferred_element_type=jnp.float32)


def slice_kernel(count, parts, rank, *refs):
    normed_refs, cot_refs = refs[:count], refs[count : 2 * count]
    gate_up, down = refs[2 * count : 2 * count + 2]
    outs = refs[2 * count + 2 : 2 * count + 2 + parts]
    normed, cot, wide, narrow, pieces, sems = refs[2 * count + 2 + parts :]
    padded = down.shape[0]
    tokens, width = normed.shape
    _, units, rows = outs[0].shape
    f32, bf16 = jnp.float32, jnp.bfloat16
    waits = fetch(normed_refs, normed, sems, 0) + fetch(cot_refs, cot, sems, count)
    for copy in waits:
        copy.wait()
    chunk = 256

    def forward(step, carry):
        at = pl.ds(pl.multiple_of(step * chunk, chunk), chunk)
        pre = product(gate_up[...], normed[at, :], ((1,), (1,)))
        act = product(down[...], cot[at, :], ((1,), (1,))).astype(bf16).astype(f32)
        gate, up = pre[:padded], pre[padded:]
        sigmoid = jax.nn.sigmoid(gate)
        wide[:padded, at] = (act * up * sigmoid * (1.0 + gate * (1.0 - sigmoid))).astype(bf16)
        wide[padded:, at] = (act * gate * sigmoid).astype(bf16)
        narrow[:, at] = (gate * sigmoid * up).astype(bf16)
        return carry

    lax.fori_loop(0, tokens // chunk, forward, 0)
    block = 2 * rows if (2 * rows) % 128 == 0 else width
    per = block // rows

    def backward(step, carry):
        at = pl.ds(pl.multiple_of(step * block, block), block)
        both = product(wide[...], normed[:, at], ((1,), (0,))).astype(bf16)
        last = product(narrow[...], cot[:, at], ((1,), (0,))).astype(bf16)
        for k in range(per):
            cols = slice(k * rows, (k + 1) * rows)
            pieces[step * per + k, 0] = both[:units, cols]
            pieces[step * per + k, 1] = both[padded : padded + units, cols]
            pieces[step * per + k, 2] = last[:units, cols]
        return carry

    lax.fori_loop(0, width // block, backward, 0)
    for k in range(parts):
        outs[k][...] = pieces[rank[0] ^ k]


def slice_grads(normed_blocks, cot_blocks, gate_up, down, rank, parts, units):
    count = len(normed_blocks)
    padded, width = down.shape
    tokens = sum(block.shape[0] for block in normed_blocks)
    rows = width // parts
    bf16 = jnp.bfloat16
    return pl.pallas_call(
        functools.partial(slice_kernel, count, parts),
        out_shape=[jax.ShapeDtypeStruct((3, units, rows), bf16)] * parts,
        in_specs=[SMEM] + [ANY] * (2 * count) + [VMEM, VMEM],
        out_specs=[VMEM] * parts,
        scratch_shapes=[
            pltpu.VMEM((tokens, width), bf16),
            pltpu.VMEM((tokens, width), bf16),
            pltpu.VMEM((2 * padded, tokens), bf16),
            pltpu.VMEM((padded, tokens), bf16),
            pltpu.VMEM((parts, 3, units, rows), bf16),
            pltpu.SemaphoreType.DMA((2 * count,)),
        ],
        name="slice_grads",
    )(rank.reshape(1), *normed_blocks, *cot_blocks, gate_up, down)


def place_kernel(rank, *refs):
    parts = len(refs) - 4
    pieces, (gate_out, up_out, down_out, buffer) = refs[:parts], refs[parts:]
    units = pieces[0].shape[1]
    for k in range(parts):
        buffer[rank[0] ^ k] = pieces[k][...]
    for j in range(parts):
        gate_out[:, j * units : (j + 1) * units] = buffer[j, 0].astype(jnp.float32).T
        up_out[:, j * units : (j + 1) * units] = buffer[j, 1].astype(jnp.float32).T
        down_out[j * units : (j + 1) * units, :] = buffer[j, 2].astype(jnp.float32)


def place(pieces, rank):
    parts = len(pieces)
    _, units, rows = pieces[0].shape
    wide = jax.ShapeDtypeStruct((rows, parts * units), jnp.float32)
    tall = jax.ShapeDtypeStruct((parts * units, rows), jnp.float32)
    return pl.pallas_call(
        place_kernel,
        out_shape=(wide, wide, tall),
        in_specs=[SMEM] + [VMEM] * parts,
        out_specs=(VMEM, VMEM, VMEM),
        scratch_shapes=[pltpu.VMEM((parts,) + pieces[0].shape, jnp.bfloat16)],
        name="place",
    )(rank.reshape(1), *pieces)


def outer_kernel(left_count, right_count, *refs):
    left_refs = refs[:left_count]
    right_refs = refs[left_count : left_count + right_count]
    out, left, right, sems = refs[left_count + right_count :]
    waits = fetch(left_refs, left, sems, 0) + fetch(right_refs, right, sems, left_count)
    for copy in waits:
        copy.wait()
    out[...] = product(left[...], right[...], ((0,), (0,)))


def outer(left_blocks, right_blocks):
    tokens = sum(block.shape[0] for block in left_blocks)
    left_width, right_width = left_blocks[0].shape[1], right_blocks[0].shape[1]
    counts = (len(left_blocks), len(right_blocks))
    return pl.pallas_call(
        functools.partial(outer_kernel, *counts),
        out_shape=jax.ShapeDtypeStruct((left_width, right_width), jnp.float32),
        in_specs=[ANY] * sum(counts),
        out_specs=VMEM,
        scratch_shapes=[
            pltpu.VMEM((tokens, left_width), jnp.bfloat16),
            pltpu.VMEM((tokens, right_width), jnp.bfloat16),
            pltpu.SemaphoreType.DMA((sum(counts),)),
        ],
        name="outer",
    )(*left_blocks, *right_blocks)


def local(
    block_input,
    segments,
    positions,
    cotangent,
    gain_attn,
    w_query,
    b_query,
    w_key,
    b_key,
    w_value,
    b_value,
    w_out,
    gain_mlp,
    w_gate,
    w_up,
    w_down,
):
    bf16 = jnp.bfloat16
    f32 = jnp.float32
    dp = lax.axis_size("dp")
    tp = lax.axis_size("tensor")
    dp_rank = lax.axis_index("dp")
    tp_rank = lax.axis_index("tensor")
    row_count = block_input.shape[0]
    own_rows = row_count // tp
    width = block_input.shape[1]
    local_heads = w_query.shape[1] // HD
    score_scale = 1.0 / math.sqrt(HD)
    head_start = tp_rank * local_heads // (H // KVH) * HD
    slice_rows = width // dp

    def exchange_columns(values):
        blocks = []
        for k in [*range(0, dp, 2), *range(1, dp, 2)]:
            block = lax.dynamic_slice_in_dim(values, (dp_rank ^ k) * slice_rows, slice_rows, 1)
            blocks.append(swap(block, "dp", k) if k else block)
        return blocks

    def dot(a, b):
        return jnp.dot(a, b, preferred_element_type=f32)

    def own_block(values):
        return lax.dynamic_slice_in_dim(values, tp_rank * own_rows, own_rows, 0)

    def reduce_tensor(partial):
        sent = partial.astype(bf16)
        total = own_block(partial)
        for k in range(1, tp):
            block = lax.dynamic_slice_in_dim(sent, (tp_rank ^ k) * own_rows, own_rows, 0)
            total = total + swap(block, "tensor", k).astype(f32)
        return total

    cot = cotangent
    cot_blocks = gather_dp(cot)

    key_own = lax.dynamic_slice_in_dim(w_key, head_start, HD, 1)
    value_own = lax.dynamic_slice_in_dim(w_value, head_start, HD, 1)
    key_bias = lax.dynamic_slice_in_dim(b_key, head_start, HD, 0)
    value_bias = lax.dynamic_slice_in_dim(b_value, head_start, HD, 0)
    input_float = block_input.astype(f32)
    rscale_attn = lax.rsqrt(jnp.mean(input_float * input_float, axis=1, keepdims=True) + eps)
    normed_attn = (input_float * rscale_attn * gain_attn).astype(bf16)
    queries = dot(normed_attn, w_query) + b_query
    keys_pre = dot(normed_attn, key_own) + key_bias
    values_pre = dot(normed_attn, value_own) + value_bias
    cosine, sine_table = rope_tables(positions)
    query_rot = rope_apply(queries.reshape(row_count, local_heads, HD), cosine, sine_table).astype(bf16)
    key_rot = rope_apply(keys_pre.reshape(row_count, 1, HD), cosine, sine_table)[:, 0].astype(bf16)
    value_heads = values_pre.astype(bf16)
    order = jnp.arange(row_count)
    allowed = (
        (segments[:, None] == segments[None, :])
        & (order[None, :] <= order[:, None])
        & (order[None, :] // SEQ == order[:, None] // SEQ)
    )
    scores = jnp.einsum("thd,ud->htu", query_rot, key_rot, preferred_element_type=f32) * score_scale
    masked = jnp.where(allowed[None], scores, -1e30)
    row_top = jnp.max(masked, axis=2, keepdims=True)
    log_total = row_top + jnp.log(jnp.sum(jnp.exp(masked - row_top), axis=2, keepdims=True))
    probabilities = jnp.exp(masked - log_total)
    rounded_probs = probabilities.astype(bf16)
    heads_out = jnp.einsum("htu,ud->thd", rounded_probs, value_heads, preferred_element_type=f32).astype(bf16)
    heads_flat = heads_out.reshape(row_count, local_heads * HD)
    attention = dot(heads_flat, w_out)
    attention = reduce_tensor(attention)
    heads_blocks = gather_dp(heads_flat)
    normed_slice = exchange_columns(normed_attn)

    d_act = lax.dot_general(cot, w_down, (((1,), (1,)), ((), ())), preferred_element_type=f32)
    d_act = lax.optimization_barrier(d_act.astype(bf16))

    units = w_gate.shape[1] // dp
    padding = ((0, -units % 16), (0, 0))
    gate_slice = lax.dynamic_slice_in_dim(w_gate, dp_rank * units, units, 1).T
    up_slice = lax.dynamic_slice_in_dim(w_up, dp_rank * units, units, 1).T
    down_slice = lax.dynamic_slice_in_dim(w_down, dp_rank * units, units, 0)
    gate_up = jnp.concatenate([jnp.pad(gate_slice, padding), jnp.pad(up_slice, padding)])
    down_slice = jnp.pad(down_slice, padding)

    input_own = own_block(input_float)
    rscale_own = own_block(rscale_attn)
    hidden = input_own + attention
    rscale_mlp = lax.rsqrt(jnp.mean(hidden * hidden, axis=1, keepdims=True) + eps)
    normed_own = (hidden * rscale_mlp * gain_mlp).astype(bf16)
    normed_mlp = arrange(normed_own, "tensor", tp_rank, bf16)
    normed_blocks = gather_dp(normed_mlp)

    gate_pre = dot(normed_mlp, w_gate)
    up_pre = dot(normed_mlp, w_up)
    act_float = d_act.astype(f32)
    sigmoid_gate = jax.nn.sigmoid(gate_pre)
    activated = (gate_pre * sigmoid_gate * up_pre).astype(bf16)
    d_gate = (act_float * up_pre * sigmoid_gate * (1.0 + gate_pre * (1.0 - sigmoid_gate))).astype(bf16)
    d_up = (act_float * gate_pre * sigmoid_gate).astype(bf16)
    mlp_partial_grad = dot(d_gate, w_gate.T) + dot(d_up, w_up.T)
    d_normed_mlp = reduce_tensor(mlp_partial_grad)
    out_partial = lax.optimization_barrier(dot(activated, w_down))
    grad_gain_mlp = jnp.sum(d_normed_mlp * hidden * rscale_mlp, axis=0)
    d_hidden = own_block(cot).astype(f32) + norm_back(hidden, rscale_mlp, gain_mlp, d_normed_mlp)
    d_hidden_own = d_hidden.astype(bf16)
    d_hidden_b = arrange(d_hidden_own, "tensor", tp_rank, bf16)
    output_own = hidden + reduce_tensor(out_partial)
    output = arrange(output_own.astype(bf16), "tensor", tp_rank, f32)

    pieces = slice_grads(normed_blocks, cot_blocks, gate_up, down_slice, dp_rank, dp, units)
    pieces = [swap(piece, "dp", k) if k else piece for k, piece in enumerate(pieces)]
    summed_gate, summed_up, summed_down = place(pieces, dp_rank)
    d_hidden_slices = exchange_columns(d_hidden_b)
    summed_out = outer(heads_blocks, d_hidden_slices)

    d_heads = dot(d_hidden_b, w_out.T).astype(bf16).reshape(row_count, local_heads, HD)
    d_probs = jnp.einsum("thd,ud->htu", d_heads, value_heads, preferred_element_type=f32)
    delta = jnp.sum(d_heads.astype(f32) * heads_out.astype(f32), axis=2)
    d_scores = (probabilities * (d_probs - delta.T[:, :, None]) * score_scale).astype(bf16)
    d_qrot = jnp.einsum("htu,ud->thd", d_scores, key_rot, preferred_element_type=f32)
    d_krot = jnp.einsum("htu,thd->uhd", d_scores, query_rot, preferred_element_type=f32)
    d_vhead = jnp.einsum("htu,thd->uhd", rounded_probs, d_heads, preferred_element_type=f32)
    d_query = rope_back(d_qrot, cosine, sine_table)
    d_key = rope_back(d_krot, cosine, sine_table)
    query_grad = d_query.astype(bf16).reshape(row_count, local_heads * HD)
    key_grad = jnp.sum(d_key.astype(bf16).astype(f32), axis=1).astype(bf16)
    value_grad = jnp.sum(d_vhead.astype(bf16).astype(f32), axis=1).astype(bf16)
    attn_partial_grad = dot(query_grad, w_query.T) + dot(key_grad, key_own.T) + dot(value_grad, value_own.T)
    d_normed_attn = reduce_tensor(attn_partial_grad)
    factor_blocks = gather_dp(jnp.concatenate([query_grad, key_grad, value_grad], axis=1))
    grad_gain_attn = jnp.sum(d_normed_attn * input_own * rscale_own, axis=0)
    d_input_own = d_hidden + norm_back(input_own, rscale_own, gain_attn, d_normed_attn)
    d_input = arrange(d_input_own.astype(bf16), "tensor", tp_rank, f32)

    products = outer(normed_slice, factor_blocks)
    summed_query = products[:, : local_heads * HD]
    kv_products = products[:, local_heads * HD :]
    kv_rows = slice_rows // tp
    kv_total = [jnp.zeros((kv_rows, 2 * HD), f32) for _ in range(KVH)]
    for k in range(tp):
        block = lax.dynamic_slice_in_dim(kv_products, (tp_rank ^ k) * kv_rows, kv_rows, 0)
        block = swap(block, "tensor", k) if k else block
        source_head = (tp_rank ^ k) * local_heads // (H // KVH)
        for head in range(KVH):
            kv_total[head] = kv_total[head] + jnp.where(source_head == head, block, 0.0)
    summed_key = jnp.concatenate([total[:, :HD] for total in kv_total], axis=1)
    summed_value = jnp.concatenate([total[:, HD:] for total in kv_total], axis=1)

    bias_query = lax.dynamic_update_slice(
        jnp.zeros((H * HD,), f32),
        jnp.sum(d_query, axis=0).reshape(local_heads * HD),
        (tp_rank * local_heads * HD,),
    )
    bias_key = lax.dynamic_update_slice(
        jnp.zeros((KVH * HD,), f32), jnp.sum(d_key, axis=(0, 1)), (head_start,)
    )
    bias_value = lax.dynamic_update_slice(
        jnp.zeros((KVH * HD,), f32), jnp.sum(d_vhead, axis=(0, 1)), (head_start,)
    )
    small = jnp.concatenate([grad_gain_attn, grad_gain_mlp, bias_query, bias_key, bias_value]).reshape(-1, HD)
    for axis, size in (("dp", dp), ("tensor", tp)):
        step = 1
        while step < size:
            small = small + swap(small, axis, step)
            step *= 2
    small = small.reshape(-1)
    ends = [0, width, 2 * width, 2 * width + H * HD, 2 * width + (H + KVH) * HD, 2 * width + (H + 2 * KVH) * HD]
    gain_attn_sum, gain_mlp_sum, bias_query_sum, bias_key_sum, bias_value_sum = (
        small[a:b] for a, b in zip(ends[:-1], ends[1:])
    )
    return (
        output,
        d_input,
        gain_attn_sum,
        summed_query,
        bias_query_sum,
        summed_key,
        bias_key_sum,
        summed_value,
        bias_value_sum,
        summed_out,
        gain_mlp_sum,
        summed_gate,
        summed_up,
        summed_down,
    )


def solution(mesh):
    return jax.shard_map(
        local,
        mesh=mesh,
        in_specs=(
            P("dp", None),
            P("dp"),
            P("dp"),
            P("dp", None),
            P(),
            P(None, "tensor"),
            P("tensor"),
            P(),
            P(),
            P(),
            P(),
            P("tensor", None),
            P(),
            P(None, "tensor"),
            P(None, "tensor"),
            P("tensor", None),
        ),
        out_specs=(
            P("dp", None),
            P("dp", None),
            P(),
            P("dp", "tensor"),
            P(),
            P(("dp", "tensor"), None),
            P(),
            P(("dp", "tensor"), None),
            P(),
            P("tensor", "dp"),
            P(),
            P("dp", "tensor"),
            P("dp", "tensor"),
            P("tensor", "dp"),
        ),
        check_vma=False,
    )
```

```python
import functools
import math

import jax
import jax.numpy as jnp
from jax import lax
from jax.experimental import pallas as pl
from jax.experimental.pallas import tpu as pltpu
from jax.sharding import PartitionSpec as P


H = 12
KVH = 2
HD = 128
SEQ = 192


eps = 1e-06
theta = 1000000.0


def rope_tables(positions):
    exponent = jnp.arange(0, HD, 2).astype(jnp.float32) / HD
    frequency = jnp.power(jnp.float32(theta), -exponent)
    angles = positions.astype(jnp.float32)[:, None] * frequency[None, :]
    cosine = jnp.concatenate([jnp.cos(angles), jnp.cos(angles)], axis=1)
    sine_table = jnp.concatenate([jnp.sin(angles), jnp.sin(angles)], axis=1)
    return (cosine, sine_table)


def rotate(values):
    first_half = values[..., : HD // 2]
    second = values[..., HD // 2 :]
    return jnp.concatenate([-second, first_half], axis=-1)


def rope_apply(values, cosine, sine_table):
    return values * cosine[:, None, :] + rotate(values) * sine_table[:, None, :]


def rope_back(gradient, cosine, sine_table):
    return gradient * cosine[:, None, :] - rotate(gradient * sine_table[:, None, :])


def norm_back(values, rscale, gain, upstream):
    scaled = gain * upstream
    return rscale * (
        scaled - values * rscale * rscale * jnp.mean(scaled * values, axis=1, keepdims=True)
    )


def swap(values, axis, step):
    size = lax.axis_size(axis)
    return lax.ppermute(values, axis, [(rank, rank ^ step) for rank in range(size)])


def turn(values, first):
    steps = (2, 4) if first else (4, 2)
    return lax.ppermute(values, "dp", [(rank, rank ^ steps[rank % 2]) for rank in range(8)])


def gather_dp(own):
    parts = lax.axis_size("dp")
    if parts == 8:
        along_x = swap(own, "dp", 2)
        along_y = swap(own, "dp", 4)
        onward = jnp.where(lax.axis_index("dp") % 2 == 0, along_y, along_x)
        chips = [own, along_x, along_y, turn(onward, True)]
    else:
        chips = [own]
        step = 2
        while step < parts:
            chips = chips + [swap(chip, "dp", step) for chip in chips]
            step *= 2
    blocks = []
    for chip in chips:
        blocks += [chip, swap(chip, "dp", 1)]
    return blocks


VMEM = pl.BlockSpec(memory_space=pltpu.VMEM)
SMEM = pl.BlockSpec(memory_space=pltpu.SMEM)
ANY = pl.BlockSpec(memory_space=pl.ANY)


def arrange_kernel(rank, *refs):
    blocks, out = refs[:-1], refs[-1]
    size = blocks[0].shape[0]
    for k, block in enumerate(blocks):
        start = pl.multiple_of((rank[0] ^ k) * size, size)
        out[pl.ds(start, size), :] = block[...].astype(out.dtype)


def arrange(own, axis, rank, dtype):
    parts = lax.axis_size(axis)
    blocks = [own] + [swap(own, axis, k) for k in range(1, parts)]
    size, width = own.shape
    return pl.pallas_call(
        arrange_kernel,
        out_shape=jax.ShapeDtypeStruct((parts * size, width), dtype),
        in_specs=[SMEM] + [VMEM] * parts,
        out_specs=VMEM,
        name="arrange",
    )(rank.reshape(1), *blocks)


def fetch(sources, target, sems, first):
    copies = []
    row = 0
    for k, source in enumerate(sources):
        rows = source.shape[0]
        copy = pltpu.make_async_copy(source, target.at[pl.ds(row, rows)], sems.at[first + k])
        copy.start()
        copies.append(copy)
        row += rows
    return copies


def product(a, b, dims):
    return lax.dot_general(a, b, (dims, ((), ())), preferred_element_type=jnp.float32)


def slice_kernel(count, parts, rank, *refs):
    normed_refs, cot_refs = refs[:count], refs[count : 2 * count]
    gate_up, down = refs[2 * count : 2 * count + 2]
    keep, give, normed, cot, wide, narrow, pieces, sems = refs[2 * count + 2 :]
    padded = down.shape[0]
    tokens, width = normed.shape
    rows = width // parts
    f32, bf16 = jnp.float32, jnp.bfloat16
    waits = fetch(normed_refs, normed, sems, 0) + fetch(cot_refs, cot, sems, count)
    for copy in waits:
        copy.wait()
    chunk = 256

    def forward(step, carry):
        at = pl.ds(pl.multiple_of(step * chunk, chunk), chunk)
        pre = product(gate_up[...], normed[at, :], ((1,), (1,)))
        act = product(down[...], cot[at, :], ((1,), (1,))).astype(bf16).astype(f32)
        gate, up = pre[:padded], pre[padded:]
        sigmoid = jax.nn.sigmoid(gate)
        wide[:padded, at] = (act * up * sigmoid * (1.0 + gate * (1.0 - sigmoid))).astype(bf16)
        wide[padded:, at] = (act * gate * sigmoid).astype(bf16)
        narrow[:, at] = (gate * sigmoid * up).astype(bf16)
        return carry

    lax.fori_loop(0, tokens // chunk, forward, 0)
    block = 2 * rows if (2 * rows) % 128 == 0 else width
    per = block // rows

    def backward(step, carry):
        at = pl.ds(pl.multiple_of(step * block, block), block)
        both = product(wide[...], normed[:, at], ((1,), (0,))).astype(bf16)
        last = product(narrow[...], cot[:, at], ((1,), (0,))).astype(bf16)
        for k in range(per):
            cols = slice(k * rows, (k + 1) * rows)
            pieces[step * per + k, : 2 * padded] = both[:, cols]
            pieces[step * per + k, 2 * padded :] = last[:, cols]
        return carry

    lax.fori_loop(0, width // block, backward, 0)
    for k in range(parts // 2):
        cols = slice((k % 2) * rows, (k % 2 + 1) * rows)
        keep[k // 2, :, cols] = pieces[rank[0] ^ (2 * k)]
        give[k // 2, :, cols] = pieces[rank[0] ^ (2 * k + 1)]


def slice_grads(normed_blocks, cot_blocks, gate_up, down, rank, parts):
    count = len(normed_blocks)
    padded, width = down.shape
    tokens = sum(block.shape[0] for block in normed_blocks)
    rows = width // parts
    bf16 = jnp.bfloat16
    return pl.pallas_call(
        functools.partial(slice_kernel, count, parts),
        out_shape=[jax.ShapeDtypeStruct((parts // 4, 3 * padded, 2 * rows), bf16)] * 2,
        in_specs=[SMEM] + [ANY] * (2 * count) + [VMEM, VMEM],
        out_specs=[VMEM] * 2,
        scratch_shapes=[
            pltpu.VMEM((tokens, width), bf16),
            pltpu.VMEM((tokens, width), bf16),
            pltpu.VMEM((2 * padded, tokens), bf16),
            pltpu.VMEM((padded, tokens), bf16),
            pltpu.VMEM((parts, 3 * padded, rows), bf16),
            pltpu.SemaphoreType.DMA((2 * count,)),
        ],
        name="slice_grads",
    )(rank.reshape(1), *normed_blocks, *cot_blocks, gate_up, down)


def pack_kernel(rank, keep, given, own, partner, *refs):
    messages, own_cols, partner_cols = refs[:-2], refs[-2], refs[-1]
    parts, _, rows = own_cols.shape
    size = keep.shape[1]
    for j in range(parts):
        own_cols[j] = own[:, j * rows : (j + 1) * rows]
        partner_cols[j] = partner[:, j * rows : (j + 1) * rows]
    for k, message in enumerate(messages):
        cols = slice((k % 2) * rows, (k % 2 + 1) * rows)
        message[:size, :rows] = keep[k // 2, :, cols]
        message[:size, rows:] = given[k // 2, :, cols]
        message[size:, :rows] = own_cols[rank[0] ^ (2 * k)]
        message[size:, rows:] = partner_cols[rank[0] ^ (2 * k)]


def pack(keep, given, own, partner, rank):
    pairs, size, wide = keep.shape
    tokens = own.shape[0]
    bf16 = jnp.bfloat16
    return pl.pallas_call(
        pack_kernel,
        out_shape=[jax.ShapeDtypeStruct((size + tokens, wide), bf16)] * (2 * pairs),
        in_specs=[SMEM] + [VMEM] * 4,
        out_specs=[VMEM] * (2 * pairs),
        scratch_shapes=[pltpu.VMEM((4 * pairs, tokens, wide // 2), bf16)] * 2,
        name="pack",
    )(rank.reshape(1), keep, given, own, partner)


def place_kernel(padded, rank, *refs):
    messages, (gate_out, up_out, down_out, buffer) = refs[:-4], refs[-4:]
    parts = 2 * len(messages)
    units = gate_out.shape[1] // parts
    rows = gate_out.shape[0]
    size = 3 * padded
    for k, message in enumerate(messages):
        buffer[rank[0] ^ (2 * k)] = message[:size, :rows]
        buffer[rank[0] ^ (2 * k + 1)] = message[:size, rows:]
    for j in range(parts):
        for part, out in enumerate((gate_out, up_out, down_out)):
            piece = buffer[j, part * padded : (part + 1) * padded].astype(jnp.float32).T
            out[:, j * units : (j + 1) * units] = piece[:, :units]


def place(messages, rank, units, padded):
    parts = 2 * len(messages)
    rows = messages[0].shape[1] // 2
    wide = jax.ShapeDtypeStruct((rows, parts * units), jnp.float32)
    return pl.pallas_call(
        functools.partial(place_kernel, padded),
        out_shape=(wide, wide, wide),
        in_specs=[SMEM] + [VMEM] * len(messages),
        out_specs=(VMEM, VMEM, VMEM),
        scratch_shapes=[pltpu.VMEM((parts, 3 * padded, rows), jnp.bfloat16)],
        name="place",
    )(rank.reshape(1), *messages)


def outer_kernel(left_count, *refs):
    left_refs, right_refs, (out, left, right, sems) = refs[:left_count], refs[left_count:-4], refs[-4:]
    for copy in fetch(left_refs, left, sems, 0) + fetch(right_refs, right, sems, left_count):
        copy.wait()
    out[...] = product(left[...], right[...], ((0,), (0,)))


def outer(left_blocks, right_blocks):
    tokens = sum(block.shape[0] for block in right_blocks)
    left_width, right_width = left_blocks[0].shape[1], right_blocks[0].shape[1]
    count = len(left_blocks) + len(right_blocks)
    return pl.pallas_call(
        functools.partial(outer_kernel, len(left_blocks)),
        out_shape=jax.ShapeDtypeStruct((left_width, right_width), jnp.float32),
        in_specs=[ANY] * count,
        out_specs=VMEM,
        scratch_shapes=[
            pltpu.VMEM((tokens, left_width), jnp.bfloat16),
            pltpu.VMEM((tokens, right_width), jnp.bfloat16),
            pltpu.SemaphoreType.DMA((count,)),
        ],
        name="outer",
    )(*left_blocks, *right_blocks)


def outer_message_kernel(first_row, count, *refs):
    messages, right_refs, (out, left, right, sems) = refs[:count], refs[count:-4], refs[-4:]
    waits = fetch(right_refs, right, sems, 0)
    tokens = messages[0].shape[0] - first_row
    width = left.shape[1]
    for k, message in enumerate(messages):
        left[2 * k * tokens : (2 * k + 1) * tokens] = message[first_row:, :width]
        left[(2 * k + 1) * tokens : (2 * k + 2) * tokens] = message[first_row:, width:]
    for copy in waits:
        copy.wait()
    out[...] = product(left[...], right[...], ((0,), (0,)))


def outer_message(messages, first_row, right_blocks):
    tokens = sum(block.shape[0] for block in right_blocks)
    left_width, right_width = messages[0].shape[1] // 2, right_blocks[0].shape[1]
    return pl.pallas_call(
        functools.partial(outer_message_kernel, first_row, len(messages)),
        out_shape=jax.ShapeDtypeStruct((left_width, right_width), jnp.float32),
        in_specs=[VMEM] * len(messages) + [ANY] * len(right_blocks),
        out_specs=VMEM,
        scratch_shapes=[
            pltpu.VMEM((tokens, left_width), jnp.bfloat16),
            pltpu.VMEM((tokens, right_width), jnp.bfloat16),
            pltpu.SemaphoreType.DMA((len(right_blocks),)),
        ],
        name="outer",
    )(*messages, *right_blocks)


def local(
    block_input,
    segments,
    positions,
    cotangent,
    gain_attn,
    w_query,
    b_query,
    w_key,
    b_key,
    w_value,
    b_value,
    w_out,
    gain_mlp,
    w_gate,
    w_up,
    w_down,
):
    bf16 = jnp.bfloat16
    f32 = jnp.float32
    dp = lax.axis_size("dp")
    tp = lax.axis_size("tensor")
    dp_rank = lax.axis_index("dp")
    tp_rank = lax.axis_index("tensor")
    row_count = block_input.shape[0]
    own_rows = row_count // tp
    width = block_input.shape[1]
    local_heads = w_query.shape[1] // HD
    score_scale = 1.0 / math.sqrt(HD)
    head_start = tp_rank * local_heads // (H // KVH) * HD
    slice_rows = width // dp

    def exchange_columns(values):
        blocks = []
        for k in range(dp):
            block = lax.dynamic_slice_in_dim(values, (dp_rank ^ k) * slice_rows, slice_rows, 1)
            blocks.append(swap(block, "dp", k) if k else block)
        return blocks

    def dot(a, b):
        return jnp.dot(a, b, preferred_element_type=f32)

    def own_block(values):
        return lax.dynamic_slice_in_dim(values, tp_rank * own_rows, own_rows, 0)

    def reduce_tensor(partial):
        sent = partial.astype(bf16)
        total = own_block(partial)
        for k in range(1, tp):
            block = lax.dynamic_slice_in_dim(sent, (tp_rank ^ k) * own_rows, own_rows, 0)
            total = total + swap(block, "tensor", k).astype(f32)
        return total

    cot = cotangent
    cot_blocks = gather_dp(cot)

    key_own = lax.dynamic_slice_in_dim(w_key, head_start, HD, 1)
    value_own = lax.dynamic_slice_in_dim(w_value, head_start, HD, 1)
    key_bias = lax.dynamic_slice_in_dim(b_key, head_start, HD, 0)
    value_bias = lax.dynamic_slice_in_dim(b_value, head_start, HD, 0)
    input_float = block_input.astype(f32)
    rscale_attn = lax.rsqrt(jnp.mean(input_float * input_float, axis=1, keepdims=True) + eps)
    normed_attn = (input_float * rscale_attn * gain_attn).astype(bf16)
    queries = dot(normed_attn, w_query) + b_query
    keys_pre = dot(normed_attn, key_own) + key_bias
    values_pre = dot(normed_attn, value_own) + value_bias
    cosine, sine_table = rope_tables(positions)
    query_rot = rope_apply(queries.reshape(row_count, local_heads, HD), cosine, sine_table).astype(bf16)
    key_rot = rope_apply(keys_pre.reshape(row_count, 1, HD), cosine, sine_table)[:, 0].astype(bf16)
    value_heads = values_pre.astype(bf16)
    order = jnp.arange(row_count)
    allowed = (
        (segments[:, None] == segments[None, :])
        & (order[None, :] <= order[:, None])
        & (order[None, :] // SEQ == order[:, None] // SEQ)
    )
    scores = jnp.einsum("thd,ud->htu", query_rot, key_rot, preferred_element_type=f32) * score_scale
    masked = jnp.where(allowed[None], scores, -1e30)
    row_top = jnp.max(masked, axis=2, keepdims=True)
    log_total = row_top + jnp.log(jnp.sum(jnp.exp(masked - row_top), axis=2, keepdims=True))
    probabilities = jnp.exp(masked - log_total)
    rounded_probs = probabilities.astype(bf16)
    heads_out = jnp.einsum("htu,ud->thd", rounded_probs, value_heads, preferred_element_type=f32).astype(bf16)
    heads_flat = heads_out.reshape(row_count, local_heads * HD)
    attention = dot(heads_flat, w_out)
    attention = reduce_tensor(attention)
    heads_blocks = gather_dp(heads_flat)
    normed_slice = exchange_columns(normed_attn)

    d_act = lax.dot_general(cot, w_down, (((1,), (1,)), ((), ())), preferred_element_type=f32)
    d_act = lax.optimization_barrier(d_act.astype(bf16))

    units = w_gate.shape[1] // dp
    padding = ((0, -units % 16), (0, 0))
    gate_slice = lax.dynamic_slice_in_dim(w_gate, dp_rank * units, units, 1).T
    up_slice = lax.dynamic_slice_in_dim(w_up, dp_rank * units, units, 1).T
    down_slice = lax.dynamic_slice_in_dim(w_down, dp_rank * units, units, 0)
    gate_up = jnp.concatenate([jnp.pad(gate_slice, padding), jnp.pad(up_slice, padding)])
    down_slice = jnp.pad(down_slice, padding)

    input_own = own_block(input_float)
    rscale_own = own_block(rscale_attn)
    hidden = input_own + attention
    rscale_mlp = lax.rsqrt(jnp.mean(hidden * hidden, axis=1, keepdims=True) + eps)
    normed_own = (hidden * rscale_mlp * gain_mlp).astype(bf16)
    normed_mlp = arrange(normed_own, "tensor", tp_rank, bf16)
    normed_blocks = gather_dp(normed_mlp)

    gate_pre = dot(normed_mlp, w_gate)
    up_pre = dot(normed_mlp, w_up)
    act_float = d_act.astype(f32)
    sigmoid_gate = jax.nn.sigmoid(gate_pre)
    activated = (gate_pre * sigmoid_gate * up_pre).astype(bf16)
    d_gate = (act_float * up_pre * sigmoid_gate * (1.0 + gate_pre * (1.0 - sigmoid_gate))).astype(bf16)
    d_up = (act_float * gate_pre * sigmoid_gate).astype(bf16)
    mlp_partial_grad = dot(d_gate, w_gate.T) + dot(d_up, w_up.T)
    d_normed_mlp = reduce_tensor(mlp_partial_grad)
    out_partial = lax.optimization_barrier(dot(activated, w_down))
    grad_gain_mlp = jnp.sum(d_normed_mlp * hidden * rscale_mlp, axis=0)
    d_hidden = own_block(cot).astype(f32) + norm_back(hidden, rscale_mlp, gain_mlp, d_normed_mlp)
    d_hidden_own = d_hidden.astype(bf16)
    d_hidden_b = arrange(d_hidden_own, "tensor", tp_rank, bf16)
    out_total = reduce_tensor(out_partial)

    keep, give = slice_grads(normed_blocks, cot_blocks, gate_up, down_slice, dp_rank, dp)
    given = swap(give, "dp", 1)
    partner_hidden = swap(d_hidden_b, "dp", 1)
    packed = pack(keep, given, d_hidden_b, partner_hidden, dp_rank)
    messages = [packed[0]]
    for k in range(1, dp // 2):
        if dp == 8 and k == 3:
            messages.append(turn(turn(packed[k], True), False))
        else:
            messages.append(swap(packed[k], "dp", 2 * k))
    summed_gate, summed_up, down_columns = place(messages, dp_rank, units, down_slice.shape[0])
    summed_out = outer_message(messages, keep.shape[1], heads_blocks).T

    d_heads = dot(d_hidden_b, w_out.T).astype(bf16).reshape(row_count, local_heads, HD)
    d_probs = jnp.einsum("thd,ud->htu", d_heads, value_heads, preferred_element_type=f32)
    delta = jnp.sum(d_heads.astype(f32) * heads_out.astype(f32), axis=2)
    d_scores = (probabilities * (d_probs - delta.T[:, :, None]) * score_scale).astype(bf16)
    d_qrot = jnp.einsum("htu,ud->thd", d_scores, key_rot, preferred_element_type=f32)
    d_krot = jnp.einsum("htu,thd->uhd", d_scores, query_rot, preferred_element_type=f32)
    d_vhead = jnp.einsum("htu,thd->uhd", rounded_probs, d_heads, preferred_element_type=f32)
    d_query = rope_back(d_qrot, cosine, sine_table)
    d_key = rope_back(d_krot, cosine, sine_table)
    query_grad = d_query.astype(bf16).reshape(row_count, local_heads * HD)
    key_grad = jnp.sum(d_key.astype(bf16).astype(f32), axis=1).astype(bf16)
    value_grad = jnp.sum(d_vhead.astype(bf16).astype(f32), axis=1).astype(bf16)
    attn_partial_grad = dot(query_grad, w_query.T) + dot(key_grad, key_own.T) + dot(value_grad, value_own.T)
    d_normed_attn = reduce_tensor(attn_partial_grad)
    factor_blocks = gather_dp(jnp.concatenate([query_grad, key_grad, value_grad], axis=1))
    grad_gain_attn = jnp.sum(d_normed_attn * input_own * rscale_own, axis=0)
    d_input_own = d_hidden + norm_back(input_own, rscale_own, gain_attn, d_normed_attn)
    d_input_b = lax.optimization_barrier(d_input_own.astype(bf16))
    d_input = arrange(d_input_b, "tensor", tp_rank, f32)
    out_total, _ = lax.optimization_barrier((out_total, d_input_b))
    output = arrange((hidden + out_total).astype(bf16), "tensor", tp_rank, f32)

    products = outer(normed_slice, factor_blocks)
    summed_query = products[:, : local_heads * HD]
    kv_products = products[:, local_heads * HD :]
    kv_rows = slice_rows // tp
    kv_total = [jnp.zeros((kv_rows, 2 * HD), f32) for _ in range(KVH)]
    for k in range(tp):
        block = lax.dynamic_slice_in_dim(kv_products, (tp_rank ^ k) * kv_rows, kv_rows, 0)
        block = swap(block, "tensor", k) if k else block
        source_head = (tp_rank ^ k) * local_heads // (H // KVH)
        for head in range(KVH):
            kv_total[head] = kv_total[head] + jnp.where(source_head == head, block, 0.0)
    summed_key = jnp.concatenate([total[:, :HD] for total in kv_total], axis=1)
    summed_value = jnp.concatenate([total[:, HD:] for total in kv_total], axis=1)

    bias_query = lax.dynamic_update_slice(
        jnp.zeros((H * HD,), f32),
        jnp.sum(d_query, axis=0).reshape(local_heads * HD),
        (tp_rank * local_heads * HD,),
    )
    bias_key = lax.dynamic_update_slice(
        jnp.zeros((KVH * HD,), f32), jnp.sum(d_key, axis=(0, 1)), (head_start,)
    )
    bias_value = lax.dynamic_update_slice(
        jnp.zeros((KVH * HD,), f32), jnp.sum(d_vhead, axis=(0, 1)), (head_start,)
    )
    small = jnp.concatenate([grad_gain_attn, grad_gain_mlp, bias_query, bias_key, bias_value]).reshape(-1, HD)
    for axis, size in (("dp", dp), ("tensor", tp)):
        step = 1
        while step < size:
            small = small + swap(small, axis, step)
            step *= 2
    small = small.reshape(-1)
    ends = [0, width, 2 * width, 2 * width + H * HD, 2 * width + (H + KVH) * HD, 2 * width + (H + 2 * KVH) * HD]
    gain_attn_sum, gain_mlp_sum, bias_query_sum, bias_key_sum, bias_value_sum = (
        small[a:b] for a, b in zip(ends[:-1], ends[1:])
    )
    return (
        output,
        d_input,
        gain_attn_sum,
        summed_query,
        bias_query_sum,
        summed_key,
        bias_key_sum,
        summed_value,
        bias_value_sum,
        summed_out,
        gain_mlp_sum,
        summed_gate,
        summed_up,
        down_columns.T,
    )


def solution(mesh):
    return jax.shard_map(
        local,
        mesh=mesh,
        in_specs=(
            P("dp", None),
            P("dp"),
            P("dp"),
            P("dp", None),
            P(),
            P(None, "tensor"),
            P("tensor"),
            P(),
            P(),
            P(),
            P(),
            P("tensor", None),
            P(),
            P(None, "tensor"),
            P(None, "tensor"),
            P("tensor", None),
        ),
        out_specs=(
            P("dp", None),
            P("dp", None),
            P(),
            P("dp", "tensor"),
            P(),
            P(("dp", "tensor"), None),
            P(),
            P(("dp", "tensor"), None),
            P(),
            P("tensor", "dp"),
            P(),
            P("dp", "tensor"),
            P("dp", "tensor"),
            P("tensor", "dp"),
        ),
        check_vma=False,
    )
```

```python
import functools
import math

import jax
import jax.numpy as jnp
from jax import lax
from jax.experimental import pallas as pl
from jax.experimental.pallas import tpu as pltpu
from jax.sharding import PartitionSpec as P


H = 12
KVH = 2
HD = 128
SEQ = 192


eps = 1e-06
theta = 1000000.0


def rope_tables(positions):
    exponent = jnp.arange(0, HD, 2).astype(jnp.float32) / HD
    frequency = jnp.power(jnp.float32(theta), -exponent)
    angles = positions.astype(jnp.float32)[:, None] * frequency[None, :]
    cosine = jnp.concatenate([jnp.cos(angles), jnp.cos(angles)], axis=1)
    sine_table = jnp.concatenate([jnp.sin(angles), jnp.sin(angles)], axis=1)
    return (cosine, sine_table)


def rotate(values):
    first_half = values[..., : HD // 2]
    second = values[..., HD // 2 :]
    return jnp.concatenate([-second, first_half], axis=-1)


def rope_apply(values, cosine, sine_table):
    return values * cosine[:, None, :] + rotate(values) * sine_table[:, None, :]


def rope_back(gradient, cosine, sine_table):
    return gradient * cosine[:, None, :] - rotate(gradient * sine_table[:, None, :])


def norm_back(values, rscale, gain, upstream):
    scaled = gain * upstream
    return rscale * (
        scaled - values * rscale * rscale * jnp.mean(scaled * values, axis=1, keepdims=True)
    )


def swap(values, axis, step):
    size = lax.axis_size(axis)
    return lax.ppermute(values, axis, [(rank, rank ^ step) for rank in range(size)])


def turn(values, first):
    steps = (2, 4) if first else (4, 2)
    return lax.ppermute(values, "dp", [(rank, rank ^ steps[rank % 2]) for rank in range(8)])


def gather_dp(own):
    parts = lax.axis_size("dp")
    if parts == 8:
        along_x = swap(own, "dp", 2)
        along_y = swap(own, "dp", 4)
        onward = jnp.where(lax.axis_index("dp") % 2 == 0, along_y, along_x)
        chips = [own, along_x, along_y, turn(onward, True)]
    else:
        chips = [own]
        step = 2
        while step < parts:
            chips = chips + [swap(chip, "dp", step) for chip in chips]
            step *= 2
    blocks = []
    for chip in chips:
        blocks += [chip, swap(chip, "dp", 1)]
    return blocks


VMEM = pl.BlockSpec(memory_space=pltpu.VMEM)
SMEM = pl.BlockSpec(memory_space=pltpu.SMEM)
ANY = pl.BlockSpec(memory_space=pl.ANY)


def arrange_kernel(rank, *refs):
    blocks, out = refs[:-1], refs[-1]
    size = blocks[0].shape[0]
    for k, block in enumerate(blocks):
        start = pl.multiple_of((rank[0] ^ k) * size, size)
        out[pl.ds(start, size), :] = block[...].astype(out.dtype)


def arrange(own, axis, rank, dtype):
    parts = lax.axis_size(axis)
    blocks = [own] + [swap(own, axis, k) for k in range(1, parts)]
    size, width = own.shape
    return pl.pallas_call(
        arrange_kernel,
        out_shape=jax.ShapeDtypeStruct((parts * size, width), dtype),
        in_specs=[SMEM] + [VMEM] * parts,
        out_specs=VMEM,
        name="arrange",
    )(rank.reshape(1), *blocks)


def fetch(sources, target, sems, first):
    copies = []
    row = 0
    for k, source in enumerate(sources):
        rows = source.shape[0]
        copy = pltpu.make_async_copy(source, target.at[pl.ds(row, rows)], sems.at[first + k])
        copy.start()
        copies.append(copy)
        row += rows
    return copies


def product(a, b, dims):
    return lax.dot_general(a, b, (dims, ((), ())), preferred_element_type=jnp.float32)


def slice_kernel(count, parts, rank, *refs):
    normed_refs, cot_refs = refs[:count], refs[count : 2 * count]
    gate_up, down = refs[2 * count : 2 * count + 2]
    keep, give, normed, cot, wide, narrow, pieces, sems = refs[2 * count + 2 :]
    padded = down.shape[0]
    tokens, width = normed.shape
    rows = width // parts
    f32, bf16 = jnp.float32, jnp.bfloat16
    normed_waits, cot_waits = fetch(normed_refs, normed, sems, 0), fetch(cot_refs, cot, sems, count)
    chunk = 256
    first = tokens // chunk // 2

    def forward(step, carry):
        at = pl.ds(pl.multiple_of(step * chunk, chunk), chunk)
        pre = product(gate_up[...], normed[at, :], ((1,), (1,)))
        act = product(down[...], cot[at, :], ((1,), (1,))).astype(bf16).astype(f32)
        gate, up = pre[:padded], pre[padded:]
        sigmoid = jax.nn.sigmoid(gate)
        wide[:padded, at] = (act * up * sigmoid * (1.0 + gate * (1.0 - sigmoid))).astype(bf16)
        wide[padded:, at] = (act * gate * sigmoid).astype(bf16)
        narrow[:, at] = (gate * sigmoid * up).astype(bf16)
        return carry

    for copy in normed_waits[: count // 2] + cot_waits[: count // 2]:
        copy.wait()
    lax.fori_loop(0, first, forward, 0)
    for copy in normed_waits[count // 2 :] + cot_waits[count // 2 :]:
        copy.wait()
    lax.fori_loop(first, tokens // chunk, forward, 0)
    block = 2 * rows if (2 * rows) % 128 == 0 else width
    per = block // rows

    def backward(step, carry):
        at = pl.ds(pl.multiple_of(step * block, block), block)
        both = product(wide[...], normed[:, at], ((1,), (0,))).astype(bf16)
        last = product(narrow[...], cot[:, at], ((1,), (0,))).astype(bf16)
        for k in range(per):
            cols = slice(k * rows, (k + 1) * rows)
            pieces[step * per + k, : 2 * padded] = both[:, cols]
            pieces[step * per + k, 2 * padded :] = last[:, cols]
        return carry

    lax.fori_loop(0, width // block, backward, 0)
    for k in range(parts // 2):
        cols = slice((k % 2) * rows, (k % 2 + 1) * rows)
        keep[k // 2, :, cols] = pieces[rank[0] ^ (2 * k)]
        give[k // 2, :, cols] = pieces[rank[0] ^ (2 * k + 1)]


def slice_grads(normed_blocks, cot_blocks, gate_up, down, rank, parts):
    count = len(normed_blocks)
    padded, width = down.shape
    tokens = sum(block.shape[0] for block in normed_blocks)
    rows = width // parts
    bf16 = jnp.bfloat16
    return pl.pallas_call(
        functools.partial(slice_kernel, count, parts),
        out_shape=[jax.ShapeDtypeStruct((parts // 4, 3 * padded, 2 * rows), bf16)] * 2,
        in_specs=[SMEM] + [ANY] * (2 * count) + [VMEM, VMEM],
        out_specs=[VMEM] * 2,
        scratch_shapes=[
            pltpu.VMEM((tokens, width), bf16),
            pltpu.VMEM((tokens, width), bf16),
            pltpu.VMEM((2 * padded, tokens), bf16),
            pltpu.VMEM((padded, tokens), bf16),
            pltpu.VMEM((parts, 3 * padded, rows), bf16),
            pltpu.SemaphoreType.DMA((2 * count,)),
        ],
        name="slice_grads",
    )(rank.reshape(1), *normed_blocks, *cot_blocks, gate_up, down)


def pack_kernel(rank, keep, given, own, partner, *refs):
    messages, own_cols, partner_cols = refs[:-2], refs[-2], refs[-1]
    parts, _, rows = own_cols.shape
    size = keep.shape[1]
    for j in range(parts):
        own_cols[j] = own[:, j * rows : (j + 1) * rows]
        partner_cols[j] = partner[:, j * rows : (j + 1) * rows]
    for k, message in enumerate(messages):
        cols = slice((k % 2) * rows, (k % 2 + 1) * rows)
        message[:size, :rows] = keep[k // 2, :, cols]
        message[:size, rows:] = given[k // 2, :, cols]
        message[size:, :rows] = own_cols[rank[0] ^ (2 * k)]
        message[size:, rows:] = partner_cols[rank[0] ^ (2 * k)]


def pack(keep, given, own, partner, rank):
    pairs, size, wide = keep.shape
    tokens = own.shape[0]
    bf16 = jnp.bfloat16
    return pl.pallas_call(
        pack_kernel,
        out_shape=[jax.ShapeDtypeStruct((size + tokens, wide), bf16)] * (2 * pairs),
        in_specs=[SMEM] + [VMEM] * 4,
        out_specs=[VMEM] * (2 * pairs),
        scratch_shapes=[pltpu.VMEM((4 * pairs, tokens, wide // 2), bf16)] * 2,
        name="pack",
    )(rank.reshape(1), keep, given, own, partner)


def place_kernel(padded, rank, *refs):
    messages, (gate_out, up_out, down_out, buffer) = refs[:-4], refs[-4:]
    parts = 2 * len(messages)
    units = gate_out.shape[1] // parts
    rows = gate_out.shape[0]
    size = 3 * padded
    for k, message in enumerate(messages):
        buffer[rank[0] ^ (2 * k)] = message[:size, :rows]
        buffer[rank[0] ^ (2 * k + 1)] = message[:size, rows:]
    for j in range(parts):
        for part, out in enumerate((gate_out, up_out, down_out)):
            piece = buffer[j, part * padded : (part + 1) * padded].astype(jnp.float32).T
            out[:, j * units : (j + 1) * units] = piece[:, :units]


def place(messages, rank, units, padded):
    parts = 2 * len(messages)
    rows = messages[0].shape[1] // 2
    wide = jax.ShapeDtypeStruct((rows, parts * units), jnp.float32)
    return pl.pallas_call(
        functools.partial(place_kernel, padded),
        out_shape=(wide, wide, wide),
        in_specs=[SMEM] + [VMEM] * len(messages),
        out_specs=(VMEM, VMEM, VMEM),
        scratch_shapes=[pltpu.VMEM((parts, 3 * padded, rows), jnp.bfloat16)],
        name="place",
    )(rank.reshape(1), *messages)


def outer_kernel(left_count, *refs):
    left_refs, right_refs, (out, left, right, sems) = refs[:left_count], refs[left_count:-4], refs[-4:]
    for copy in fetch(left_refs, left, sems, 0) + fetch(right_refs, right, sems, left_count):
        copy.wait()
    out[...] = product(left[...], right[...], ((0,), (0,)))


def outer(left_blocks, right_blocks):
    tokens = sum(block.shape[0] for block in right_blocks)
    left_width, right_width = left_blocks[0].shape[1], right_blocks[0].shape[1]
    count = len(left_blocks) + len(right_blocks)
    return pl.pallas_call(
        functools.partial(outer_kernel, len(left_blocks)),
        out_shape=jax.ShapeDtypeStruct((left_width, right_width), jnp.float32),
        in_specs=[ANY] * count,
        out_specs=VMEM,
        scratch_shapes=[
            pltpu.VMEM((tokens, left_width), jnp.bfloat16),
            pltpu.VMEM((tokens, right_width), jnp.bfloat16),
            pltpu.SemaphoreType.DMA((count,)),
        ],
        name="outer",
    )(*left_blocks, *right_blocks)


def outer_message_kernel(first_row, count, *refs):
    messages, right_refs, (out, left, right, sems) = refs[:count], refs[count:-4], refs[-4:]
    waits = fetch(right_refs, right, sems, 0)
    tokens = messages[0].shape[0] - first_row
    width = left.shape[1]
    for k, message in enumerate(messages):
        left[2 * k * tokens : (2 * k + 1) * tokens] = message[first_row:, :width]
        left[(2 * k + 1) * tokens : (2 * k + 2) * tokens] = message[first_row:, width:]
    for copy in waits:
        copy.wait()
    out[...] = product(left[...], right[...], ((0,), (0,)))


def outer_message(messages, first_row, right_blocks):
    tokens = sum(block.shape[0] for block in right_blocks)
    left_width, right_width = messages[0].shape[1] // 2, right_blocks[0].shape[1]
    return pl.pallas_call(
        functools.partial(outer_message_kernel, first_row, len(messages)),
        out_shape=jax.ShapeDtypeStruct((left_width, right_width), jnp.float32),
        in_specs=[VMEM] * len(messages) + [ANY] * len(right_blocks),
        out_specs=VMEM,
        scratch_shapes=[
            pltpu.VMEM((tokens, left_width), jnp.bfloat16),
            pltpu.VMEM((tokens, right_width), jnp.bfloat16),
            pltpu.SemaphoreType.DMA((len(right_blocks),)),
        ],
        name="outer",
    )(*messages, *right_blocks)


def local(
    block_input,
    segments,
    positions,
    cotangent,
    gain_attn,
    w_query,
    b_query,
    w_key,
    b_key,
    w_value,
    b_value,
    w_out,
    gain_mlp,
    w_gate,
    w_up,
    w_down,
):
    bf16 = jnp.bfloat16
    f32 = jnp.float32
    dp = lax.axis_size("dp")
    tp = lax.axis_size("tensor")
    dp_rank = lax.axis_index("dp")
    tp_rank = lax.axis_index("tensor")
    row_count = block_input.shape[0]
    own_rows = row_count // tp
    width = block_input.shape[1]
    local_heads = w_query.shape[1] // HD
    score_scale = 1.0 / math.sqrt(HD)
    head_start = tp_rank * local_heads // (H // KVH) * HD
    slice_rows = width // dp

    def exchange_columns(values):
        blocks = []
        for k in range(dp):
            block = lax.dynamic_slice_in_dim(values, (dp_rank ^ k) * slice_rows, slice_rows, 1)
            blocks.append(swap(block, "dp", k) if k else block)
        return blocks

    def dot(a, b):
        return jnp.dot(a, b, preferred_element_type=f32)

    def own_block(values):
        return lax.dynamic_slice_in_dim(values, tp_rank * own_rows, own_rows, 0)

    def reduce_tensor(partial):
        sent = partial.astype(bf16)
        total = own_block(partial)
        for k in range(1, tp):
            block = lax.dynamic_slice_in_dim(sent, (tp_rank ^ k) * own_rows, own_rows, 0)
            total = total + swap(block, "tensor", k).astype(f32)
        return total

    cot = cotangent
    cot_blocks = gather_dp(cot)

    key_own = lax.dynamic_slice_in_dim(w_key, head_start, HD, 1)
    value_own = lax.dynamic_slice_in_dim(w_value, head_start, HD, 1)
    key_bias = lax.dynamic_slice_in_dim(b_key, head_start, HD, 0)
    value_bias = lax.dynamic_slice_in_dim(b_value, head_start, HD, 0)
    input_float = block_input.astype(f32)
    rscale_attn = lax.rsqrt(jnp.mean(input_float * input_float, axis=1, keepdims=True) + eps)
    normed_attn = (input_float * rscale_attn * gain_attn).astype(bf16)
    queries = dot(normed_attn, w_query) + b_query
    keys_pre = dot(normed_attn, key_own) + key_bias
    values_pre = dot(normed_attn, value_own) + value_bias
    cosine, sine_table = rope_tables(positions)
    query_rot = rope_apply(queries.reshape(row_count, local_heads, HD), cosine, sine_table).astype(bf16)
    key_rot = rope_apply(keys_pre.reshape(row_count, 1, HD), cosine, sine_table)[:, 0].astype(bf16)
    value_heads = values_pre.astype(bf16)
    order = jnp.arange(row_count)
    allowed = (
        (segments[:, None] == segments[None, :])
        & (order[None, :] <= order[:, None])
        & (order[None, :] // SEQ == order[:, None] // SEQ)
    )
    scores = jnp.einsum("thd,ud->htu", query_rot, key_rot, preferred_element_type=f32) * score_scale
    masked = jnp.where(allowed[None], scores, -1e30)
    row_top = jnp.max(masked, axis=2, keepdims=True)
    log_total = row_top + jnp.log(jnp.sum(jnp.exp(masked - row_top), axis=2, keepdims=True))
    probabilities = jnp.exp(masked - log_total)
    rounded_probs = probabilities.astype(bf16)
    heads_out = jnp.einsum("htu,ud->thd", rounded_probs, value_heads, preferred_element_type=f32).astype(bf16)
    heads_flat = heads_out.reshape(row_count, local_heads * HD)
    attention = dot(heads_flat, w_out)
    attention = reduce_tensor(attention)
    heads_blocks = gather_dp(heads_flat)
    normed_slice = exchange_columns(normed_attn)

    d_act = lax.dot_general(cot, w_down, (((1,), (1,)), ((), ())), preferred_element_type=f32)
    d_act = lax.optimization_barrier(d_act.astype(bf16))

    units = w_gate.shape[1] // dp
    padding = ((0, -units % 16), (0, 0))
    gate_slice = lax.dynamic_slice_in_dim(w_gate, dp_rank * units, units, 1).T
    up_slice = lax.dynamic_slice_in_dim(w_up, dp_rank * units, units, 1).T
    down_slice = lax.dynamic_slice_in_dim(w_down, dp_rank * units, units, 0)
    gate_up = jnp.concatenate([jnp.pad(gate_slice, padding), jnp.pad(up_slice, padding)])
    down_slice = jnp.pad(down_slice, padding)

    input_own = own_block(input_float)
    rscale_own = own_block(rscale_attn)
    hidden = input_own + attention
    rscale_mlp = lax.rsqrt(jnp.mean(hidden * hidden, axis=1, keepdims=True) + eps)
    normed_own = (hidden * rscale_mlp * gain_mlp).astype(bf16)
    normed_mlp = arrange(normed_own, "tensor", tp_rank, bf16)
    normed_blocks = gather_dp(normed_mlp)

    gate_pre = dot(normed_mlp, w_gate)
    up_pre = dot(normed_mlp, w_up)
    act_float = d_act.astype(f32)
    sigmoid_gate = jax.nn.sigmoid(gate_pre)
    activated = (gate_pre * sigmoid_gate * up_pre).astype(bf16)
    d_gate = (act_float * up_pre * sigmoid_gate * (1.0 + gate_pre * (1.0 - sigmoid_gate))).astype(bf16)
    d_up = (act_float * gate_pre * sigmoid_gate).astype(bf16)
    mlp_partial_grad = dot(d_gate, w_gate.T) + dot(d_up, w_up.T)
    d_normed_mlp = reduce_tensor(mlp_partial_grad)
    out_partial = lax.optimization_barrier(dot(activated, w_down))
    grad_gain_mlp = jnp.sum(d_normed_mlp * hidden * rscale_mlp, axis=0)
    d_hidden = own_block(cot).astype(f32) + norm_back(hidden, rscale_mlp, gain_mlp, d_normed_mlp)
    d_hidden_own = d_hidden.astype(bf16)
    d_hidden_b = arrange(d_hidden_own, "tensor", tp_rank, bf16)
    out_total = reduce_tensor(out_partial)

    keep, give = slice_grads(normed_blocks, cot_blocks, gate_up, down_slice, dp_rank, dp)
    given = swap(give, "dp", 1)
    partner_hidden = swap(d_hidden_b, "dp", 1)
    packed = pack(keep, given, d_hidden_b, partner_hidden, dp_rank)
    messages = [packed[0]]
    for k in range(1, dp // 2):
        if dp == 8 and k == 3:
            messages.append(turn(turn(packed[k], True), False))
        else:
            messages.append(swap(packed[k], "dp", 2 * k))
    summed_gate, summed_up, down_columns = place(messages, dp_rank, units, down_slice.shape[0])
    summed_out = outer_message(messages, keep.shape[1], heads_blocks).T

    d_heads = dot(d_hidden_b, w_out.T).astype(bf16).reshape(row_count, local_heads, HD)
    d_probs = jnp.einsum("thd,ud->htu", d_heads, value_heads, preferred_element_type=f32)
    delta = jnp.sum(d_heads.astype(f32) * heads_out.astype(f32), axis=2)
    d_scores = (probabilities * (d_probs - delta.T[:, :, None]) * score_scale).astype(bf16)
    d_qrot = jnp.einsum("htu,ud->thd", d_scores, key_rot, preferred_element_type=f32)
    d_krot = jnp.einsum("htu,thd->uhd", d_scores, query_rot, preferred_element_type=f32)
    d_vhead = jnp.einsum("htu,thd->uhd", rounded_probs, d_heads, preferred_element_type=f32)
    d_query = rope_back(d_qrot, cosine, sine_table)
    d_key = rope_back(d_krot, cosine, sine_table)
    query_grad = d_query.astype(bf16).reshape(row_count, local_heads * HD)
    key_grad = jnp.sum(d_key.astype(bf16).astype(f32), axis=1).astype(bf16)
    value_grad = jnp.sum(d_vhead.astype(bf16).astype(f32), axis=1).astype(bf16)
    attn_partial_grad = dot(query_grad, w_query.T) + dot(key_grad, key_own.T) + dot(value_grad, value_own.T)
    d_normed_attn = reduce_tensor(attn_partial_grad)
    factor_blocks = gather_dp(jnp.concatenate([query_grad, key_grad, value_grad], axis=1))
    d_input_own = d_hidden + norm_back(input_own, rscale_own, gain_attn, d_normed_attn)
    d_input_b = lax.optimization_barrier(d_input_own.astype(bf16))
    d_input = arrange(d_input_b, "tensor", tp_rank, f32)
    out_total, _ = lax.optimization_barrier((out_total, d_input_b))
    output = arrange((hidden + out_total).astype(bf16), "tensor", tp_rank, f32)

    products = outer(normed_slice, factor_blocks)
    summed_query = products[:, : local_heads * HD]
    kv_products = products[:, local_heads * HD :]
    kv_rows = slice_rows // tp
    kv_total = [jnp.zeros((kv_rows, 2 * HD), f32) for _ in range(KVH)]
    for k in range(tp):
        block = lax.dynamic_slice_in_dim(kv_products, (tp_rank ^ k) * kv_rows, kv_rows, 0)
        block = swap(block, "tensor", k) if k else block
        source_head = (tp_rank ^ k) * local_heads // (H // KVH)
        for head in range(KVH):
            kv_total[head] = kv_total[head] + jnp.where(source_head == head, block, 0.0)
    summed_key = jnp.concatenate([total[:, :HD] for total in kv_total], axis=1)
    summed_value = jnp.concatenate([total[:, HD:] for total in kv_total], axis=1)

    grad_gain_attn = jnp.sum(attn_partial_grad * input_float * rscale_attn, axis=0)
    bias_query = lax.dynamic_update_slice(
        jnp.zeros((H * HD,), f32),
        jnp.sum(d_query, axis=0).reshape(local_heads * HD),
        (tp_rank * local_heads * HD,),
    )
    bias_key = lax.dynamic_update_slice(
        jnp.zeros((KVH * HD,), f32), jnp.sum(d_key, axis=(0, 1)), (head_start,)
    )
    bias_value = lax.dynamic_update_slice(
        jnp.zeros((KVH * HD,), f32), jnp.sum(d_vhead, axis=(0, 1)), (head_start,)
    )
    small = jnp.concatenate([grad_gain_attn, grad_gain_mlp, bias_query, bias_key, bias_value]).reshape(-1, HD)
    for axis, size in (("dp", dp), ("tensor", tp)):
        step = 1
        while step < size:
            small = small + swap(small, axis, step)
            step *= 2
    small = small.reshape(-1)
    ends = [0, width, 2 * width, 2 * width + H * HD, 2 * width + (H + KVH) * HD, 2 * width + (H + 2 * KVH) * HD]
    gain_attn_sum, gain_mlp_sum, bias_query_sum, bias_key_sum, bias_value_sum = (
        small[a:b] for a, b in zip(ends[:-1], ends[1:])
    )
    return (
        output,
        d_input,
        gain_attn_sum,
        summed_query,
        bias_query_sum,
        summed_key,
        bias_key_sum,
        summed_value,
        bias_value_sum,
        summed_out,
        gain_mlp_sum,
        summed_gate,
        summed_up,
        down_columns.T,
    )


def solution(mesh):
    return jax.shard_map(
        local,
        mesh=mesh,
        in_specs=(
            P("dp", None),
            P("dp"),
            P("dp"),
            P("dp", None),
            P(),
            P(None, "tensor"),
            P("tensor"),
            P(),
            P(),
            P(),
            P(),
            P("tensor", None),
            P(),
            P(None, "tensor"),
            P(None, "tensor"),
            P("tensor", None),
        ),
        out_specs=(
            P("dp", None),
            P("dp", None),
            P(),
            P("dp", "tensor"),
            P(),
            P(("dp", "tensor"), None),
            P(),
            P(("dp", "tensor"), None),
            P(),
            P("tensor", "dp"),
            P(),
            P("dp", "tensor"),
            P("dp", "tensor"),
            P("tensor", "dp"),
        ),
        check_vma=False,
    )
```
